32 devices in a mesh: xy: 8 (over y, x, core), gz: 4 (over z).
Axes of the slice: x: 2, y: 2, z: 4, core: 2. Of those that a mesh axis runs over, the one named last changes fastest.
Arguments:
- features: bfloat16 [8, 2, 4, 64, 128], P('xy', None, 'gz'), may hold values from -6 to 6
- cotangent: bfloat16 [8, 2, 4, 64, 128], P('xy', None, 'gz'), may hold values from -6 to 6
- positions: float32 [8, 2, 4, 3, 64], P('xy', None, 'gz'), may hold values from 0 to 1
- counts: int32 [8, 2, 4], P('xy', None, 'gz'), may hold values from 32 to 64
- neighbour_mask: int32 [8, 2, 4, 27], P('xy', None, 'gz'), may hold values 0 or 1
- proj_weight: bfloat16 [128, 64], replicated, may hold values from -0.5 to 0.5
- out_weight: bfloat16 [64, 128], replicated, may hold values from -0.75 to 0.75
- radial_weight: float32 [8, 64], replicated, may hold values from -58 to 58
Outputs:
- updated: bfloat16 [8, 2, 4, 64, 128], P('xy', None, 'gz')
- feature_grad: bfloat16 [8, 2, 4, 64, 128], P('xy', None, 'gz')
The draws below stay inside these ranges and needn't reach their ends.
Inputs may be any that keep to these rules, and one draw needn't show every extreme that they name: `counts`: the atoms of a cell beyond its count are padding. `neighbour_mask`: entry d refers to the direction numbered as in the reference program.
All inputs are finite; a program needn't handle non-finite values. No bound on the sum of `neighbour_mask` on one device may be relied on, other than what follows from the above.
Results may differ from the reference program's by a relative error of at most 0.007.
Values may be sent and summed in bfloat16 or wider, within the bound.
A program may use at most 64 MiB of HBM per device.

```python
import jax
import jax.numpy as jnp
from jax import lax

ATOMS = 64
CH = 128
PROJ = 64
BASES = 8
NX = 8
NY = 2
NZ = 4


def draw_radial_weight(key, part):
    centres = (jnp.arange(BASES, dtype=jnp.float32) + 0.5) / BASES
    damping = jnp.maximum(jnp.square(1.0 - centres), 1.0 / 64.0)
    row_scale = (0.3 / damping)[:, None]
    sample = jax.random.truncated_normal(key, -3.0, 3.0, (BASES, PROJ), jnp.float32)
    return (sample * row_scale).astype(jnp.float32)


def with_ends(entries, rng, smallest, top_value):
    extent = entries.shape
    place = [jax.random.randint(jax.random.fold_in(rng, axis), (), 0, extent[axis]) for axis in range(len(extent))]
    entries = entries.at[tuple(place)].set(smallest)
    longest = extent.index(max(extent))
    place[longest] = (place[longest] + 1) % extent[longest]
    return entries.at[tuple(place)].set(top_value)


def block_scale(rng, dims, split, smallest, high):
    def one(axis_at, shards_of):
        steps = jax.random.uniform(jax.random.fold_in(jax.random.fold_in(rng, 6), axis_at), (shards_of,), jnp.float32, smallest / len(split), high / len(split))
        return jnp.repeat(jnp.exp(steps), dims[axis_at] // shards_of).reshape((-1,) + (1,) * (len(dims) - axis_at - 1))

    loudness = one(*split[0])
    for cut in split[1:]:
        loudness = loudness * one(*cut)
    return loudness


def centred(rng, dims, deviation, bound, pieces=(), kind=jnp.bfloat16):
    gain = block_scale(rng, dims, pieces, -0.22, 0.18) if pieces else 1.0
    entries = jax.random.normal(rng, dims, jnp.float32) * deviation * gain
    return jnp.minimum(jnp.maximum(entries, -bound), bound).astype(kind)


def setup_inputs(seed: int = 0) -> dict:
    arg_keys = jax.random.split(jax.random.key(seed), 9)
    features = centred(arg_keys[0], (NX, NY, NZ, ATOMS, CH), 1.0, 6.0, ((0, 8), (2, 4)))
    cotangent = centred(arg_keys[1], (NX, NY, NZ, ATOMS, CH), 1.0, 6.0, ((0, 8), (2, 4)))
    positions = jnp.clip(1.0 * jax.random.uniform(arg_keys[2], (NX, NY, NZ, 3, ATOMS), jnp.float32) ** block_scale(arg_keys[2], (NX, NY, NZ, 3, ATOMS), ((0, 8), (2, 4)), -0.2, 0.2), 0.0, 1.0)
    counts = with_ends(jax.random.randint(arg_keys[3], (NX, NY, NZ), ATOMS // 2, ATOMS + 1), jax.random.fold_in(arg_keys[3], 1), ATOMS // 2, ATOMS).astype(jnp.int32)
    neighbour_mask = with_ends((jax.random.randint(arg_keys[4], (NX, NY, NZ, 27), 0, 8) < 7).astype(jnp.int32), jax.random.fold_in(arg_keys[4], 1), 0, 1)
    proj_weight = centred(arg_keys[5], (CH, PROJ), CH ** -0.5, 0.5)
    out_weight = centred(arg_keys[6], (PROJ, CH), PROJ ** -0.5, 0.75)
    radial_weight = draw_radial_weight(jax.random.fold_in(arg_keys[8], 71), 0)
    return {"features": features, "cotangent": cotangent, "positions": positions, "counts": counts, "neighbour_mask": neighbour_mask, "proj_weight": proj_weight, "out_weight": out_weight, "radial_weight": radial_weight}


def offsets():
    return [(direction // 9 - 1, (direction // 3) % 3 - 1, direction % 3 - 1) for direction in range(27)]


def build_tiles(own_pos, own_valid, other_pos, other_valid, cell_gate, shift_vec, self_flag):
    separation = other_pos[:, :, None, :] + shift_vec[None, :, None, None] - own_pos[:, :, :, None]
    squared = 4.0 * jnp.sum(separation * separation, axis=1)
    atom_count = own_pos.shape[2]
    diagonal_ones = (jnp.arange(atom_count)[:, None] == jnp.arange(atom_count)[None, :]).astype(jnp.float32)
    pair_keep = own_valid[:, :, None] * other_valid[:, None, :] * cell_gate[:, None, None]
    pair_keep = pair_keep * (1.0 - self_flag * diagonal_ones)
    envelope = jnp.square(jnp.maximum(1.0 - squared, 0.0)) * pair_keep
    basis_list = [(envelope * jnp.exp(-2.0 * jnp.square(BASES * squared - which_basis - 0.5))).astype(jnp.bfloat16) for which_basis in range(BASES)]
    return jnp.stack(basis_list, axis=1)


def combine_bases(tile_set, source, radial_weight):
    per_basis = jnp.einsum("cbij,ckj->cbki", tile_set.astype(jnp.float32), source.astype(jnp.float32), precision=lax.Precision.HIGHEST)
    return jnp.einsum("cbki,bk->cki", per_basis, radial_weight, precision=lax.Precision.HIGHEST)


def gather_messages(source, positions, valid_atom, mask_float, radial_weight):
    running = jnp.zeros(source.shape, jnp.float32)
    for direction, (shift_x, shift_y, shift_z) in enumerate(offsets()):
        def shifted(values):
            return jnp.roll(values, (-shift_x, -shift_y, -shift_z), axis=(0, 1, 2))

        cell_gate = mask_float[..., direction] * shifted(mask_float)[..., 26 - direction]
        shift_vec = jnp.array([shift_x, shift_y, shift_z], jnp.float32)
        self_flag = jnp.float32(1.0 if direction == 13 else 0.0)

        def one_slab(members):
            own_pos, own_valid, other_pos, other_valid, slab_gate, slab_source = members
            cell_total = own_pos.shape[0] * own_pos.shape[1]
            tile_set = build_tiles(own_pos.reshape((cell_total,) + own_pos.shape[2:]), own_valid.reshape((cell_total,) + own_valid.shape[2:]), other_pos.reshape((cell_total,) + other_pos.shape[2:]), other_valid.reshape((cell_total,) + other_valid.shape[2:]), slab_gate.reshape(cell_total), shift_vec, self_flag)
            result = combine_bases(tile_set, slab_source.reshape((cell_total,) + slab_source.shape[2:]), radial_weight)
            return result.reshape(slab_source.shape)

        running = running + lax.map(one_slab, (positions, valid_atom, shifted(positions), shifted(valid_atom), cell_gate, shifted(source)))
    return running


def reference(features, cotangent, positions, counts, neighbour_mask, proj_weight, out_weight, radial_weight):
    highest = lax.Precision.HIGHEST
    valid_atom = (jnp.arange(ATOMS, dtype=jnp.int32)[None, None, None, :] < counts[..., None]).astype(jnp.float32)
    mask_float = neighbour_mask.astype(jnp.float32)
    projected = jnp.einsum("xyzin,nk->xyzki", features.astype(jnp.float32), proj_weight.astype(jnp.float32), precision=highest).astype(jnp.bfloat16)
    message = gather_messages(projected, positions, valid_atom, mask_float, radial_weight)
    activated = jax.nn.silu(message).astype(jnp.bfloat16)
    updated = (features.astype(jnp.float32) + jnp.einsum("xyzki,kn->xyzin", activated.astype(jnp.float32), out_weight.astype(jnp.float32), precision=highest)).astype(jnp.bfloat16)
    grad_act = jnp.einsum("xyzin,kn->xyzki", cotangent.astype(jnp.float32), out_weight.astype(jnp.float32), precision=highest)
    sigmoid_m = jax.nn.sigmoid(message)
    grad_msg = (grad_act * sigmoid_m * (1.0 + message * (1.0 - sigmoid_m))).astype(jnp.bfloat16)
    grad_proj = gather_messages(grad_msg, positions, valid_atom, mask_float, radial_weight).astype(jnp.bfloat16)
    feature_grad = (cotangent.astype(jnp.float32) + jnp.einsum("xyzki,nk->xyzin", grad_proj.astype(jnp.float32), proj_weight.astype(jnp.float32), precision=highest)).astype(jnp.bfloat16)
    return updated, feature_grad
```

```python
import functools

import jax
import jax.numpy as jnp
from jax import lax
from jax.experimental import pallas as pl
from jax.experimental.pallas import tpu as pltpu
from jax.sharding import PartitionSpec as P

MESH = pl.DeviceIdType.MESH
AXES = ("xy", "gz")
F32 = jnp.float32
BF16 = jnp.bfloat16
LOG2E = 1.4426950408889634

SAME, INNER, OUTER = 0, 1, 2
LEVEL, SOONER, LATER = 0, 1, 2
SLOTS = {1: (INNER, LEVEL), 2: (OUTER, LEVEL)}
SLOTS.update({3 + at: (at, SOONER) for at in (SAME, INNER, OUTER)})
SLOTS.update({6 + at: (at, LATER) for at in (SAME, INNER, OUTER)})
GROUPS = ((0, 1), (2, 3), (4, 5), (6, 7), (8,))
WAITS = {(0, 1): (1, 2), (2, 3): (3,), (4, 5): (4, 5), (6, 7): (6, 7), (8,): (8,)}


def nt(a, b):
    return lax.dot_general(a, b, (((1,), (1,)), ((), ())), preferred_element_type=F32)


def tn(a, b):
    return lax.dot_general(a, b, (((0,), (0,)), ((), ())), preferred_element_type=F32)


def direction(ox, oy, oz):
    return (ox + 1) * 9 + (oy + 1) * 3 + oz + 1


def basis_scale(bases):
    off = lax.broadcasted_iota(jnp.int32, (bases, 1), 0).astype(F32) - 0.5 * (bases - 1)
    return jnp.exp(-2.0 * off * off)


def kernel(
    atoms,
    bases,
    feat_hbm,
    cot_hbm,
    pos_hbm,
    counts_hbm,
    mask_hbm,
    proj_hbm,
    outw_hbm,
    radial_hbm,
    both_ref,
    feat_ref,
    cot_ref,
    pos_ref,
    counts_ref,
    mask_ref,
    proj_ref,
    outw_ref,
    radial_ref,
    packet_out,
    packet_in,
    relay,
    own_cols,
    tiles,
    weights,
    source,
    grads,
    local_sem,
    relay_sem,
    told_sem,
    send_sem,
    recv_sem,
):
    rows = feat_ref.shape[0]
    size_x, size_z = [lax.axis_size(axis) for axis in AXES]
    assert size_x % 2 == 0 and size_z >= 4
    here_x, here_z = [lax.axis_index(axis) for axis in AXES]
    first_z, second_z, last_z = here_z == 0, here_z == 1, here_z == size_z - 1

    odd_x = lax.rem(here_x, 2) == 1
    inward = jnp.where(odd_x, -1, 1)
    off_x = (0, inward, -inward)
    near_z = jnp.where(first_z, 1, -1)
    off_z = (0, near_z, -near_z)
    at_x = [here_x] + [lax.rem(here_x + off + size_x, size_x) for off in off_x[1:]]
    at_z = [here_z] + [lax.rem(here_z + off + size_z, size_z) for off in off_z[1:]]

    into_z = [0] + [
        jnp.where(jnp.where(at_z[side] == 0, 1, -1) == -off_z[side], 3, 6) for side in (SOONER, LATER)
    ]

    def slot_there(slot):
        column, level = SLOTS[slot]
        return slot if level == LEVEL else into_z[level] + column

    def device(slot):
        column, level = SLOTS[slot]
        return (at_x[column], at_z[level])

    barrier = pltpu.get_barrier_semaphore()

    def greet(column, z):
        pl.semaphore_signal(barrier, inc=1, device_id=(at_x[column], z), device_id_type=MESH)

    later_z = jnp.where(last_z, 1, at_z[LATER])
    for column in (OUTER, SAME, INNER):
        greet(column, later_z)
    greet(SAME, at_z[SOONER])

    @pl.when(jnp.logical_not(second_z))
    def _():
        greet(OUTER, at_z[SOONER])
        greet(INNER, at_z[SOONER])

    @pl.when(jnp.logical_not(jnp.logical_and(first_z, odd_x)))
    def _():
        greet(OUTER, here_z)
        greet(INNER, here_z)

    fetches = [
        pltpu.make_async_copy(far, near, local_sem.at[at])
        for at, far, near in (
            (0, mask_hbm, mask_ref),
            (1, counts_hbm, counts_ref),
            (2, pos_hbm, pos_ref),
            (3, proj_hbm, proj_ref),
            (3, feat_hbm, feat_ref),
            (4, radial_hbm, radial_ref),
            (5, outw_hbm, outw_ref),
            (5, cot_hbm, cot_ref),
        )
    ]
    for fetch in fetches:
        fetch.start()

    def fetched_pair(at):
        both = source.at[0 : 1 + rows // proj_ref.shape[0]]
        pltpu.make_async_copy(both, both, local_sem.at[at]).wait()

    with jax.named_scope("fetch"):
        for fetch in fetches[:3]:
            fetch.wait()

    lane = lax.broadcasted_iota(jnp.int32, (1, rows), 1)
    upper = lane >= atoms
    valid_lane = (lane - jnp.where(upper, atoms, 0)) < jnp.where(upper, counts_ref[1], counts_ref[0])
    valid_row = valid_lane.astype(F32)

    place = 2.0 * jnp.concatenate(
        [jnp.concatenate([pos_ref[axis], pos_ref[3 + axis]], axis=-1) for axis in range(3)], axis=0
    )

    def packet_for(ox, oz):
        listed = [
            jnp.where(
                upper,
                mask_ref[1, direction(ox, -oy, oz)].astype(F32),
                mask_ref[0, direction(ox, -oy, oz)].astype(F32),
            )
            for oy in (-1, 0, 1)
        ]
        return jnp.concatenate([place] + listed + [jnp.zeros((2, rows), F32)], axis=0)

    packet_in[0] = packet_for(0, 0)
    for slot, (column, level) in SLOTS.items():
        packet_out[slot] = packet_for(off_x[column], off_z[level])

    def held_at(kind, slot):
        return (packet_in, source, grads)[kind].at[slot]

    def remote(src, dst, send, recv, to):
        return pltpu.make_async_remote_copy(
            src_ref=src,
            dst_ref=dst,
            send_sem=send,
            recv_sem=recv,
            device_id=to,
            device_id_type=MESH,
        )

    def lands(kind, slot):
        if kind == 0:
            return slot - 1
        return 5 * kind + (3, 3, 4, 5, 5, 6, 6, 7)[slot - 1]

    def landing(kind, slot):
        level = SLOTS[slot][1]
        if level == LEVEL:
            return recv_sem.at[lands(kind, slot)]
        column = SLOTS[slot][0]
        return recv_sem.at[jnp.where(into_z[level] == 3, lands(kind, 3 + column), lands(kind, 6 + column))]

    def spread(kind, slots):
        for slot in slots:
            column, level = SLOTS[slot]
            src = packet_out.at[slot] if kind == 0 else held_at(kind, 0)
            there = slot_there(slot)
            remote(src, held_at(kind, there), send_sem.at[kind], landing(kind, slot), device(slot)).start()

    def arrived(kind, low, high):
        held = (packet_in, source, grads)[kind].at[low:high]
        remote(held, held, send_sem.at[kind], recv_sem.at[lands(kind, low)], device(1)).wait_recv()

    def sent(kind, count):
        some = (packet_in, source, grads)[kind].at[0:count]
        remote(some, some, send_sem.at[kind], recv_sem.at[0], device(1)).wait_send()

    def build(slot):
        column, level = SLOTS[slot] if slot else (SAME, LEVEL)
        ox, oz = off_x[column], off_z[level]
        packet = packet_in[slot]
        other_x = packet[0:1] + 2.0 * (ox if column == SAME else ox.astype(F32))
        other_y = packet[1:2]
        other_z = packet[2:3] + 2.0 * (oz if level == LEVEL else oz.astype(F32))
        middle_row = 4
        chunk = 32
        for c in range(2):
            cross = upper if c == 0 else jnp.logical_not(upper)
            low, same, high = (
                packet[middle_row + oy : middle_row + oy + 1]
                * mask_ref[c, direction(ox, oy, oz)].astype(F32)
                for oy in (-1, 0, 1)
            )
            gate_low = jnp.where(cross, low, same)
            gate_high = jnp.where(cross, high, same)
            move = jnp.where(cross, 2.0, 0.0)

            for first in range(c * atoms, (c + 1) * atoms, chunk):
                some = pl.ds(first, chunk)
                dx = other_x - own_cols[0, some, :]
                dy = other_y - own_cols[1, some, :]
                dz = other_z - own_cols[2, some, :]
                gate = jnp.where(dy > 0.0, gate_low, gate_high)
                dy = jnp.abs(dy) - move
                near = jnp.minimum(dx * dx + dy * dy + dz * dz, 1.0)
                room = 1.0 - near
                envelope = room * room * gate
                if slot == 0:
                    at_row = lax.broadcasted_iota(jnp.int32, (chunk, rows), 0) + first
                    at_lane = lax.broadcasted_iota(jnp.int32, (chunk, rows), 1)
                    envelope = jnp.where(at_row == at_lane, 0.0, envelope)
                half = bases // 2
                rise = (4.0 * LOG2E) * (bases * near - half)
                up, down = jnp.exp2(rise), jnp.exp2(-rise)
                high = envelope * jnp.exp2(rise * (0.5 - rise * (0.125 / LOG2E)))
                low = high * down
                for step_out in range(half):
                    if step_out:
                        high, low = high * up, low * down
                    for b, value in ((half + step_out, high), (half - 1 - step_out, low)):
                        tiles[slot * bases + b, some, :] = value.astype(BF16)

    def gathered(held, slots, total):
        values = jnp.concatenate([held[slot] for slot in slots], axis=1)
        built = [tiles[slot * bases : (slot + 1) * bases].reshape(bases * rows, rows) for slot in slots]
        sums = nt(values, jnp.concatenate(built, axis=1))
        for b in range(bases):
            term = sums[:, b * rows : (b + 1) * rows] * weights[b]
            total = term if total is None else total + term
        return total

    fetched_pair(3)
    projected = nt(proj_ref[...], feat_ref[...])
    source[0] = (projected * valid_row).astype(BF16)

    heard = jnp.where(first_z, jnp.where(odd_x, 3, 1), jnp.where(second_z, 11, 8))

    @pl.when(here_z > 1)
    def _():
        with jax.named_scope("barrier"):
            pl.semaphore_wait(barrier, heard)
        spread(0, (2, 1, 8, 6, 7, 3, 5, 4))
        spread(1, (2, 1, 8, 6, 7, 3, 5, 4))

    with jax.named_scope("own"):
        columns = jnp.concatenate([place, jnp.zeros((5, rows), F32)], axis=0).T
        for axis in range(3):
            own_cols[axis] = jnp.broadcast_to(columns[:, axis : axis + 1], (rows, rows))
        fetches[5].wait()
        radial = (radial_ref[...] * basis_scale(bases)).T
        for b in range(bases):
            weights[b] = jnp.broadcast_to(radial[:, b : b + 1], (radial.shape[0], rows))
        fetched_pair(5)
        build(0)
        grad_act = nt(outw_ref[...], cot_ref[...])

    with jax.named_scope("spread"):

        @pl.when(first_z)
        def _():
            with jax.named_scope("barrier"):
                pl.semaphore_wait(barrier, heard)
            spread(1, (3,))
            remote(packet_out.at[6:9], relay, send_sem.at[0], relay_sem, device(3)).start()
            spread(0, (3,))

            @pl.when(odd_x)
            def _():
                for slot in (2, 1):
                    pl.semaphore_signal(told_sem.at[0], inc=1, device_id=device(slot), device_id_type=MESH)

            @pl.when(jnp.logical_not(odd_x))
            def _():
                pl.semaphore_wait(told_sem.at[0], 2)

            spread(0, (2, 1))
            spread(1, (2, 1))
            with jax.named_scope("told"):
                pl.semaphore_wait(told_sem.at[1], 1)
            spread(0, (5, 4))
            spread(1, (5, 4))

        @pl.when(second_z)
        def _():
            with jax.named_scope("barrier"):
                pl.semaphore_wait(barrier, heard)
            pl.semaphore_signal(told_sem.at[1], inc=1, device_id=device(3), device_id_type=MESH)
            spread(0, (2, 1, 3, 5, 4))
            spread(1, (2, 1, 3, 5, 4))
            with jax.named_scope("relay"):
                arrived(1, 3, 4)
                remote(relay, relay, send_sem.at[0], relay_sem, device(1)).wait_recv()
            for column in (OUTER, SAME, INNER):
                to = (at_x[column], size_z - 1)
                there = 6 + column
                for kind, src in ((0, relay.at[column]), (1, held_at(1, 3))):
                    land = recv_sem.at[lands(kind, there)]
                    remote(src, held_at(kind, there), send_sem.at[kind], land, to).start()
            spread(0, (8, 6, 7))
            spread(1, (8, 6, 7))

    def take(kind, slot):
        if kind == 0:
            arrived(0, slot, slot + 1)
        elif kind == 1 and slot == 3:
            pl.when(jnp.logical_not(second_z))(lambda: arrived(1, 3, 4))
        elif slot == 8 or lands(kind, slot + 1) != lands(kind, slot):
            low = min(at for at in range(1, 9) if lands(kind, at) == lands(kind, slot))
            arrived(kind, low, slot + 1)

    message = None
    for group in GROUPS:
        for slot in group:
            if slot:
                with jax.named_scope(f"p{slot}"):
                    take(0, slot)
                with jax.named_scope("build"):
                    build(slot)
        with jax.named_scope(f"s{group[-1]}"):
            for slot in WAITS[group]:
                take(1, slot)
        with jax.named_scope("gather"):
            message = gathered(source, group, message)

    message = message * valid_row
    gate = 1.0 / (1.0 + jnp.exp(-message))
    grad_msg = grad_act * gate * (1.0 + message * (1.0 - gate)) * valid_row
    grads[0] = grad_msg.astype(BF16)
    with jax.named_scope("spread2"):
        spread(2, (8, 6, 7, 3, 5, 4, 2, 1))

    activated = (message * gate).astype(BF16)
    both_ref[0] = (feat_ref[...].astype(F32) + tn(activated, outw_ref[...])).astype(BF16)

    total = None
    for group in GROUPS:
        with jax.named_scope(f"g{group[-1]}"):
            for slot in WAITS[group]:
                take(2, slot)
        with jax.named_scope("gather2"):
            total = gathered(grads, group, total)
    grad_proj = (total * valid_row).astype(BF16)
    pulled = tn(grad_proj, proj_ref[...])
    both_ref[1] = (cot_ref[...].astype(F32) + pulled).astype(BF16)

    with jax.named_scope("sent"):
        sent(0, 8)
        sent(1, 5)
        sent(2, 8)

        @pl.when(jnp.logical_not(first_z))
        def _():
            sent(1, 3)

        @pl.when(second_z)
        def _():
            sent(0, 3)
            sent(1, 3)


def on_device(
    features, cotangent, positions, counts, neighbour_mask, proj_weight, out_weight, radial_weight
):
    shape = features.shape
    cells, atoms, channels = shape[1], shape[3], shape[4]
    bases, width = radial_weight.shape
    rows = cells * atoms
    assert shape[0] == 1 and shape[2] == 1 and cells == 2
    operands = (
        features.reshape(rows, channels),
        cotangent.reshape(rows, channels),
        positions.reshape(cells * 3, 1, atoms),
        counts.reshape(cells),
        neighbour_mask.reshape(cells, neighbour_mask.shape[-1]),
        proj_weight.T,
        out_weight,
        radial_weight,
    )
    held = [pltpu.SMEM if at in (3, 4) else pltpu.VMEM for at in range(len(operands))]
    both = pl.pallas_call(
        functools.partial(kernel, atoms, bases),
        out_shape=pltpu.VMEM((2, rows, channels), BF16),
        in_specs=[pl.BlockSpec(memory_space=pl.ANY)] * len(operands),
        out_specs=pl.BlockSpec(memory_space=pltpu.VMEM),
        scratch_shapes=[space(x.shape, x.dtype) for space, x in zip(held, operands)]
        + [
            pltpu.VMEM((9, 8, rows), F32),
            pltpu.VMEM((9, 8, rows), F32),
            pltpu.VMEM((3, 8, rows), F32),
            pltpu.VMEM((3, rows, rows), F32),
            pltpu.VMEM((9 * bases, rows, rows), BF16),
            pltpu.VMEM((bases, width, rows), F32),
            pltpu.VMEM((9, width, rows), BF16),
            pltpu.VMEM((9, width, rows), BF16),
            pltpu.SemaphoreType.DMA((6,)),
            pltpu.SemaphoreType.DMA,
            pltpu.SemaphoreType.REGULAR((2,)),
            pltpu.SemaphoreType.DMA((3,)),
            pltpu.SemaphoreType.DMA((18,)),
        ],
        compiler_params=pltpu.CompilerParams(collective_id=0, has_side_effects=True),
    )(*operands)
    return both[0].reshape(shape), both[1].reshape(shape)


def solution(mesh):
    cell = P("xy", None, "gz", None, None)
    return jax.shard_map(
        on_device,
        mesh=mesh,
        in_specs=(cell, cell, cell, P("xy", None, "gz"), P("xy", None, "gz", None), P(), P(), P()),
        out_specs=(cell, cell),
        check_vma=False,
    )
```

```python
import functools

import jax
import jax.numpy as jnp
from jax import lax
from jax.experimental import pallas as pl
from jax.experimental.pallas import tpu as pltpu
from jax.sharding import PartitionSpec as P

MESH = pl.DeviceIdType.MESH
AXES = ("xy", "gz")
F32 = jnp.float32
BF16 = jnp.bfloat16
LOG2E = 1.4426950408889634
PIECES = 4

SAME, INNER, OUTER = 0, 1, 2
LEVEL, SOONER, LATER = 0, 1, 2
SLOTS = {1: (INNER, LEVEL), 2: (OUTER, LEVEL)}
SLOTS.update({3 + at: (at, SOONER) for at in (SAME, INNER, OUTER)})
SLOTS.update({6 + at: (at, LATER) for at in (SAME, INNER, OUTER)})
STAGES = (
    ((1,), (), ()),
    ((2, 6), (1,), (0, 1)),
    ((7, 8), (2, 6), (2, 6)),
    ((), (7, 8), (7, 8)),
    ((3,), (), ()),
    ((5,), (), ()),
    ((4,), (3, 5), (3, 5)),
    ((), (4,), (4,)),
)


def nt(a, b):
    return lax.dot_general(a, b, (((1,), (1,)), ((), ())), preferred_element_type=F32)


def tn(a, b):
    return lax.dot_general(a, b, (((0,), (0,)), ((), ())), preferred_element_type=F32)


def direction(ox, oy, oz):
    return (ox + 1) * 9 + (oy + 1) * 3 + oz + 1


def basis_scale(bases):
    off = lax.broadcasted_iota(jnp.int32, (bases, 1), 0).astype(F32) - 0.5 * (bases - 1)
    return jnp.exp(-2.0 * off * off)


def kernel(
    atoms,
    bases,
    feat_hbm,
    cot_hbm,
    pos_hbm,
    counts_hbm,
    mask_hbm,
    proj_hbm,
    outw_hbm,
    radial_hbm,
    both_ref,
    feat_ref,
    cot_ref,
    pos_ref,
    counts_ref,
    mask_ref,
    proj_ref,
    outw_ref,
    radial_ref,
    packet_out,
    packet_in,
    relay,
    own_cols,
    tiles,
    weights,
    source,
    grads,
    owes,
    local_sem,
    relay_sem,
    told_sem,
    send_sem,
    recv_sem,
):
    rows = feat_ref.shape[0]
    size_x, size_z = [lax.axis_size(axis) for axis in AXES]
    assert size_x % 2 == 0 and size_z >= 4
    here_x, here_z = [lax.axis_index(axis) for axis in AXES]
    first_z, second_z, last_z = here_z == 0, here_z == 1, here_z == size_z - 1

    odd_x = lax.rem(here_x, 2) == 1
    inward = jnp.where(odd_x, -1, 1)
    off_x = (0, inward, -inward)

    def sooner_of(z):
        return jnp.where(jnp.logical_or(z == 0, z == size_z - 1), 1, -1)

    off_z = (0, sooner_of(here_z), -sooner_of(here_z))
    at_x = [here_x] + [lax.rem(here_x + off + size_x, size_x) for off in off_x[1:]]
    at_z = [here_z] + [lax.rem(here_z + off + size_z, size_z) for off in off_z[1:]]

    into_z = [0] + [
        jnp.where(sooner_of(at_z[side]) == -off_z[side], 3, 6) for side in (SOONER, LATER)
    ]

    def slot_there(slot):
        column, level = SLOTS[slot]
        return slot if level == LEVEL else into_z[level] + column

    def device(slot):
        column, level = SLOTS[slot]
        return (at_x[column], at_z[level])

    barrier = pltpu.get_barrier_semaphore()

    def greet(column, z):
        pl.semaphore_signal(barrier, inc=1, device_id=(at_x[column], z), device_id_type=MESH)

    sooner_z = jnp.where(last_z, 1, at_z[SOONER])

    @pl.when(jnp.logical_not(second_z))
    def _():
        greet(OUTER, sooner_z)
        greet(INNER, sooner_z)

    greet(SAME, sooner_z)
    for column in (OUTER, SAME, INNER):
        greet(column, at_z[LATER])

    @pl.when(jnp.logical_not(jnp.logical_and(first_z, odd_x)))
    def _():
        greet(OUTER, here_z)
        greet(INNER, here_z)

    fetches = [
        pltpu.make_async_copy(far, near, local_sem.at[at])
        for at, far, near in (
            (0, mask_hbm, mask_ref),
            (1, counts_hbm, counts_ref),
            (2, pos_hbm, pos_ref),
            (3, proj_hbm, proj_ref),
            (3, feat_hbm, feat_ref),
            (4, radial_hbm, radial_ref),
            (5, outw_hbm, outw_ref),
            (5, cot_hbm, cot_ref),
        )
    ]
    for fetch in fetches:
        fetch.start()

    def fetched_pair(at):
        both = source.at[0 : 1 + rows // proj_ref.shape[0]]
        pltpu.make_async_copy(both, both, local_sem.at[at]).wait()

    with jax.named_scope("fetch"):
        for fetch in fetches[:3]:
            fetch.wait()

    lane = lax.broadcasted_iota(jnp.int32, (1, rows), 1)
    upper = lane >= atoms
    valid_lane = (lane - jnp.where(upper, atoms, 0)) < jnp.where(upper, counts_ref[1], counts_ref[0])
    valid_row = valid_lane.astype(F32)

    place = 2.0 * jnp.concatenate(
        [jnp.concatenate([pos_ref[axis], pos_ref[3 + axis]], axis=-1) for axis in range(3)], axis=0
    )

    def packet_for(ox, oz):
        listed = [
            jnp.where(
                upper,
                mask_ref[1, direction(ox, -oy, oz)].astype(F32),
                mask_ref[0, direction(ox, -oy, oz)].astype(F32),
            )
            for oy in (-1, 0, 1)
        ]
        return jnp.concatenate([place] + listed + [jnp.zeros((2, rows), F32)], axis=0)

    packet_in[0] = packet_for(0, 0)
    for slot, (column, level) in SLOTS.items():
        packet_out[slot] = packet_for(off_x[column], off_z[level])

    def held_at(kind, slot):
        return (packet_in, source, grads)[kind].at[slot]

    def remote(src, dst, send, recv, to):
        return pltpu.make_async_remote_copy(
            src_ref=src,
            dst_ref=dst,
            send_sem=send,
            recv_sem=recv,
            device_id=to,
            device_id_type=MESH,
        )

    def lands(kind, slot):
        if kind == 0:
            return slot - 1
        return 8 + (0, 1, 2, 3, 4, 5, 6, 6)[slot - 1]

    def landing(kind, slot):
        level = SLOTS[slot][1]
        if level == LEVEL:
            return recv_sem.at[lands(kind, slot)]
        column = SLOTS[slot][0]
        return recv_sem.at[jnp.where(into_z[level] == 3, lands(kind, 3 + column), lands(kind, 6 + column))]

    def spread(kind, slots):
        for slot in slots:
            column, level = SLOTS[slot]
            src = packet_out.at[slot] if kind == 0 else held_at(kind, 0)
            there = slot_there(slot)
            remote(src, held_at(kind, there), send_sem.at[kind], landing(kind, slot), device(slot)).start()

    def arrived(kind, low, high):
        held = (packet_in, source, grads)[kind].at[low:high]
        remote(held, held, send_sem.at[kind], recv_sem.at[lands(kind, low)], device(1)).wait_recv()

    def sent(kind, count):
        some = (packet_in, source, grads)[kind].at[0:count]
        remote(some, some, send_sem.at[kind], recv_sem.at[0], device(1)).wait_send()

    def build(slot):
        column, level = SLOTS[slot] if slot else (SAME, LEVEL)
        ox, oz = off_x[column], off_z[level]
        packet = packet_in[slot]
        other_x = packet[0:1] + 2.0 * (ox if column == SAME else ox.astype(F32))
        other_y = packet[1:2]
        other_z = packet[2:3] + 2.0 * (oz if level == LEVEL else oz.astype(F32))
        chunk = 32
        half = bases // 2

        def step(first, gate_low, gate_high, move):
            some = slice(first, first + chunk)
            dx = other_x - own_cols[0, some, :]
            dy = other_y - own_cols[1, some, :]
            dz = other_z - own_cols[2, some, :]
            gate = jnp.where(dy > 0.0, gate_low, gate_high)
            dy = jnp.abs(dy) - move
            near = jnp.minimum(dx * dx + dy * dy + dz * dz, 1.0)
            room = 1.0 - near
            envelope = room * room * gate
            if slot == 0:
                at_row = lax.broadcasted_iota(jnp.int32, (chunk, rows), 0) + first
                at_lane = lax.broadcasted_iota(jnp.int32, (chunk, rows), 1)
                envelope = jnp.where(at_row == at_lane, 0.0, envelope)
            rise = (4.0 * LOG2E * bases) * near - (4.0 * LOG2E * half)
            up, down = jnp.exp2(rise), jnp.exp2(-rise)
            high = envelope * jnp.exp2(rise * (0.5 - rise * (0.125 / LOG2E)))
            low = high * down
            for step_out in range(half):
                if step_out:
                    high, low = high * up, low * down
                for b, value in ((half + step_out, high), (half - 1 - step_out, low)):
                    tiles[slot * bases + b, some, :] = value.astype(BF16)

        for c in range(2):
            cross = upper if c == 0 else jnp.logical_not(upper)
            low, same, high = (
                packet[4 + oy : 5 + oy] * mask_ref[c, direction(ox, oy, oz)].astype(F32) for oy in (-1, 0, 1)
            )
            gate_low = jnp.where(cross, low, same)
            gate_high = jnp.where(cross, high, same)
            move = jnp.where(cross, 2.0, 0.0)
            for first in range(c * atoms, (c + 1) * atoms, chunk):
                yield functools.partial(step, first, gate_low, gate_high, move)

    def gathered(slots, total, building=()):
        steps = [step for slot in building for step in build(slot)]
        values = jnp.concatenate([source[slot] for slot in slots], axis=1)
        for piece in range(PIECES):
            some = range(piece * bases // PIECES, (piece + 1) * bases // PIECES)
            built = [jnp.concatenate([tiles[slot * bases + b] for slot in slots], axis=1) for b in some]
            sums = nt(values, jnp.concatenate(built, axis=0))
            for at, b in enumerate(some):
                term = sums[:, at * rows : (at + 1) * rows] * weights[b]
                total = term if total is None else total + term
            for step in steps[piece * len(steps) // PIECES : (piece + 1) * len(steps) // PIECES]:
                step()
        return total

    def owed(value, slots):
        for slot in slots:
            built = tiles[pl.ds(slot * bases, bases)]
            some = jnp.concatenate([built[b] for b in range(bases)], axis=1)
            sums = jnp.dot(value, some, preferred_element_type=F32)
            total = None
            for b in range(bases):
                term = sums[:, b * rows : (b + 1) * rows] * weights[b]
                total = term if total is None else total + term
            owes[slot] = total.astype(BF16)

    def build_all(slot):
        for step in build(slot):
            step()

    fetched_pair(3)
    projected = nt(proj_ref[...], feat_ref[...])
    source[0] = (projected * valid_row).astype(BF16)

    heard = jnp.where(first_z, jnp.where(odd_x, 3, 1), jnp.where(second_z, 11, 8))

    @pl.when(here_z > 1)
    def _():
        with jax.named_scope("barrier"):
            pl.semaphore_wait(barrier, heard)
        spread(0, (2, 1, 8, 6, 7))
        spread(1, (2, 1, 8, 6, 7))
        spread(0, (5, 3, 4))
        spread(1, (5, 3, 4))

    with jax.named_scope("own"):
        columns = jnp.concatenate([place, jnp.zeros((5, rows), F32)], axis=0).T
        for axis in range(3):
            own_cols[axis] = jnp.broadcast_to(columns[:, axis : axis + 1], (rows, rows))
        fetches[5].wait()
        radial = (radial_ref[...] * basis_scale(bases)).T
        for b in range(bases):
            weights[b] = jnp.broadcast_to(radial[:, b : b + 1], (radial.shape[0], rows))
        fetched_pair(5)
        build_all(0)
        grad_act = nt(outw_ref[...], cot_ref[...])

    with jax.named_scope("spread"):

        @pl.when(first_z)
        def _():
            with jax.named_scope("barrier"):
                pl.semaphore_wait(barrier, heard)
            remote(packet_out.at[6:9], relay, send_sem.at[0], relay_sem, device(3)).start()
            spread(1, (3,))
            spread(0, (3,))

            @pl.when(odd_x)
            def _():
                for slot in (2, 1):
                    pl.semaphore_signal(told_sem.at[0], inc=1, device_id=device(slot), device_id_type=MESH)

            @pl.when(jnp.logical_not(odd_x))
            def _():
                pl.semaphore_wait(told_sem.at[0], 2)

            spread(0, (2, 1))
            spread(1, (2, 1))
            with jax.named_scope("told"):
                pl.semaphore_wait(told_sem.at[1], 1)
            spread(0, (5, 4))
            spread(1, (5, 4))

        @pl.when(second_z)
        def _():
            with jax.named_scope("barrier"):
                pl.semaphore_wait(barrier, heard)
            pl.semaphore_signal(told_sem.at[1], inc=1, device_id=device(3), device_id_type=MESH)
            spread(0, (2, 1, 3, 5, 4))
            spread(1, (2, 3, 5, 4, 1))

            def pass_on(kind, sources):
                for column in (OUTER, SAME, INNER):
                    there = 3 + column
                    land = recv_sem.at[lands(kind, there)]
                    to = (at_x[column], size_z - 1)
                    remote(sources[column], held_at(kind, there), send_sem.at[kind], land, to).start()

            with jax.named_scope("relay"):
                remote(relay, relay, send_sem.at[0], relay_sem, device(1)).wait_recv()
            pass_on(0, [relay.at[column] for column in range(3)])
            with jax.named_scope("relay1"):
                arrived(1, 3, 4)
            pass_on(1, [held_at(1, 3)] * 3)
            spread(0, (8, 6, 7))
            spread(1, (8, 6, 7))

    def take(kind, slot):
        if kind == 0:
            arrived(0, slot, slot + 1)
        elif kind == 1 and slot == 3:
            pl.when(jnp.logical_not(second_z))(lambda: arrived(1, 3, 4))
        elif slot == 8 or lands(kind, slot + 1) != lands(kind, slot):
            low = min(at for at in range(1, 9) if lands(kind, at) == lands(kind, slot))
            arrived(kind, low, slot + 1)

    message = None
    for at, (packets, features, group) in enumerate(STAGES):
        with jax.named_scope(f"p{at}"):
            for slot in packets:
                take(0, slot)
        with jax.named_scope(f"s{at}"):
            for slot in features:
                take(1, slot)
        with jax.named_scope("stage"):
            if group:
                message = gathered(group, message, packets)
            else:
                for slot in packets:
                    build_all(slot)

    message = message * valid_row
    gate = 0.5 + 0.5 * jnp.tanh(0.5 * message)
    grad_msg = grad_act * gate * (1.0 + message * (1.0 - gate)) * valid_row
    grad_msg = grad_msg.astype(BF16)
    for turn in range(3):
        level = jnp.where(first_z, turn, jnp.where(last_z, (1, 2, 0)[turn], (1, 0, 2)[turn]))
        to_z = jnp.where(level == SOONER, at_z[SOONER], jnp.where(level == LATER, at_z[LATER], here_z))
        there_z = jnp.where(level == SOONER, into_z[SOONER], jnp.where(level == LATER, into_z[LATER], 0))
        land = recv_sem.at[15 + there_z // 3]
        with jax.named_scope(f"owed{turn}"):
            for columns in ((OUTER,), (SAME, INNER)) if turn == 0 else ((OUTER, SAME, INNER),):
                owed(grad_msg, [3 * level + column for column in columns])
                for column in columns:

                    def send(column=column):
                        src, dst = owes.at[3 * level + column], grads.at[there_z + column]
                        remote(src, dst, send_sem.at[2], land, (at_x[column], to_z)).start()

                    if column == SAME:
                        pl.when(level != LEVEL)(send)
                    else:
                        send()

    activated = (message * gate).astype(BF16)
    both_ref[0] = (feat_ref[...].astype(F32) + tn(activated, outw_ref[...])).astype(BF16)

    total = owes[0].astype(F32)
    for low, high in ((1, 3), (3, 6), (6, 9)):
        with jax.named_scope(f"g{high - 1}"):
            held = grads.at[low:high]
            remote(held, held, send_sem.at[2], recv_sem.at[15 + low // 3], device(1)).wait_recv()
        for slot in range(low, high):
            total += grads[slot].astype(F32)
    grad_proj = (total * valid_row).astype(BF16)
    pulled = tn(grad_proj, proj_ref[...])
    both_ref[1] = (cot_ref[...].astype(F32) + pulled).astype(BF16)

    with jax.named_scope("sent"):
        sent(0, 8)
        sent(1, 5)
        sent(2, 8)

        @pl.when(jnp.logical_not(first_z))
        def _():
            sent(1, 3)

        @pl.when(second_z)
        def _():
            sent(0, 3)
            sent(1, 3)


def on_device(
    features, cotangent, positions, counts, neighbour_mask, proj_weight, out_weight, radial_weight
):
    shape = features.shape
    cells, atoms, channels = shape[1], shape[3], shape[4]
    bases, width = radial_weight.shape
    rows = cells * atoms
    assert shape[0] == 1 and shape[2] == 1 and cells == 2
    operands = (
        features.reshape(rows, channels),
        cotangent.reshape(rows, channels),
        positions.reshape(cells * 3, 1, atoms),
        counts.reshape(cells),
        neighbour_mask.reshape(cells, neighbour_mask.shape[-1]),
        proj_weight.T,
        out_weight,
        radial_weight,
    )
    held = [pltpu.SMEM if at in (3, 4) else pltpu.VMEM for at in range(len(operands))]
    both = pl.pallas_call(
        functools.partial(kernel, atoms, bases),
        out_shape=pltpu.VMEM((2, rows, channels), BF16),
        in_specs=[pl.BlockSpec(memory_space=pl.ANY)] * len(operands),
        out_specs=pl.BlockSpec(memory_space=pltpu.VMEM),
        scratch_shapes=[space(x.shape, x.dtype) for space, x in zip(held, operands)]
        + [
            pltpu.VMEM((9, 8, rows), F32),
            pltpu.VMEM((9, 8, rows), F32),
            pltpu.VMEM((3, 8, rows), F32),
            pltpu.VMEM((3, rows, rows), F32),
            pltpu.VMEM((9 * bases, rows, rows), BF16),
            pltpu.VMEM((bases, width, rows), F32),
            pltpu.VMEM((9, width, rows), BF16),
            pltpu.VMEM((9, width, rows), BF16),
            pltpu.VMEM((9, width, rows), BF16),
            pltpu.SemaphoreType.DMA((6,)),
            pltpu.SemaphoreType.DMA,
            pltpu.SemaphoreType.REGULAR((2,)),
            pltpu.SemaphoreType.DMA((3,)),
            pltpu.SemaphoreType.DMA((18,)),
        ],
        compiler_params=pltpu.CompilerParams(collective_id=0, has_side_effects=True),
    )(*operands)
    return both[0].reshape(shape), both[1].reshape(shape)


def solution(mesh):
    cell = P("xy", None, "gz", None, None)
    return jax.shard_map(
        on_device,
        mesh=mesh,
        in_specs=(cell, cell, cell, P("xy", None, "gz"), P("xy", None, "gz", None), P(), P(), P()),
        out_specs=(cell, cell),
        check_vma=False,
    )
```

```python
import functools

import jax
import jax.numpy as jnp
from jax import lax
from jax.experimental import pallas as pl
from jax.experimental.pallas import tpu as pltpu
from jax.sharding import PartitionSpec as P

MESH = pl.DeviceIdType.MESH
AXES = ("xy", "gz")
F32 = jnp.float32
BF16 = jnp.bfloat16
LOG2E = 1.4426950408889634
PIECES = 4

SAME, INNER, OUTER = 0, 1, 2
LEVEL, SOONER, LATER = 0, 1, 2
SLOTS = {1: (INNER, LEVEL), 2: (OUTER, LEVEL)}
SLOTS.update({3 + at: (at, SOONER) for at in (SAME, INNER, OUTER)})
SLOTS.update({6 + at: (at, LATER) for at in (SAME, INNER, OUTER)})
STAGES = (
    ((1,), (), ()),
    ((2,), (1,), (0, 1)),
    ((6, 7), (2,), (2,)),
    ((8,), (), ()),
    ((3,), (6, 7), (6, 7)),
    ((5,), (8,), (8,)),
    ((4,), (3, 5), (3, 5)),
    ((), (4,), (4,)),
)


def nt(a, b):
    return lax.dot_general(a, b, (((1,), (1,)), ((), ())), preferred_element_type=F32)


def tn(a, b):
    return lax.dot_general(a, b, (((0,), (0,)), ((), ())), preferred_element_type=F32)


def direction(ox, oy, oz):
    return (ox + 1) * 9 + (oy + 1) * 3 + oz + 1


def basis_scale(bases):
    off = lax.broadcasted_iota(jnp.int32, (bases, 1), 0).astype(F32) - 0.5 * (bases - 1)
    return jnp.exp(-2.0 * off * off)


def kernel(
    atoms,
    bases,
    feat_hbm,
    cot_hbm,
    pos_hbm,
    counts_hbm,
    mask_hbm,
    proj_hbm,
    outw_hbm,
    radial_hbm,
    both_ref,
    feat_ref,
    cot_ref,
    pos_ref,
    counts_ref,
    mask_ref,
    proj_ref,
    outw_ref,
    radial_ref,
    packet_out,
    packet_in,
    relay,
    own_cols,
    tiles,
    weights,
    source,
    grads,
    owes,
    local_sem,
    relay_sem,
    told_sem,
    send_sem,
    recv_sem,
):
    rows = feat_ref.shape[0]
    size_x, size_z = [lax.axis_size(axis) for axis in AXES]
    assert size_x % 2 == 0 and size_z >= 4
    here_x, here_z = [lax.axis_index(axis) for axis in AXES]
    first_z, second_z, last_z = here_z == 0, here_z == 1, here_z == size_z - 1

    odd_x = lax.rem(here_x, 2) == 1
    inward = jnp.where(odd_x, -1, 1)
    off_x = (0, inward, -inward)

    def sooner_of(z):
        return jnp.where(z == size_z - 1, 1, -1)

    off_z = (0, sooner_of(here_z), -sooner_of(here_z))
    at_x = [here_x] + [lax.rem(here_x + off + size_x, size_x) for off in off_x[1:]]
    at_z = [here_z] + [lax.rem(here_z + off + size_z, size_z) for off in off_z[1:]]

    into_z = [0] + [
        jnp.where(sooner_of(at_z[side]) == -off_z[side], 3, 6) for side in (SOONER, LATER)
    ]

    def slot_there(slot):
        column, level = SLOTS[slot]
        return slot if level == LEVEL else into_z[level] + column

    def device(slot):
        column, level = SLOTS[slot]
        return (at_x[column], at_z[level])

    barrier = pltpu.get_barrier_semaphore()

    def greet(column, z):
        pl.semaphore_signal(barrier, inc=1, device_id=(at_x[column], z), device_id_type=MESH)

    sooner_z = jnp.where(last_z, 1, at_z[SOONER])

    @pl.when(jnp.logical_not(second_z))
    def _():
        greet(OUTER, sooner_z)
        greet(INNER, sooner_z)

    greet(SAME, sooner_z)
    for column in (OUTER, SAME, INNER):
        greet(column, at_z[LATER])

    @pl.when(jnp.logical_not(jnp.logical_and(first_z, odd_x)))
    def _():
        greet(OUTER, here_z)
        greet(INNER, here_z)

    fetches = [
        pltpu.make_async_copy(far, near, local_sem.at[at])
        for at, far, near in (
            (0, mask_hbm, mask_ref),
            (1, counts_hbm, counts_ref),
            (2, pos_hbm, pos_ref),
            (3, proj_hbm, proj_ref),
            (3, feat_hbm, feat_ref),
            (4, radial_hbm, radial_ref),
            (5, outw_hbm, outw_ref),
            (5, cot_hbm, cot_ref),
        )
    ]
    for fetch in fetches:
        fetch.start()

    def fetched_pair(at):
        both = source.at[0 : 1 + rows // proj_ref.shape[0]]
        pltpu.make_async_copy(both, both, local_sem.at[at]).wait()

    with jax.named_scope("fetch"):
        for fetch in fetches[:3]:
            fetch.wait()

    lane = lax.broadcasted_iota(jnp.int32, (1, rows), 1)
    upper = lane >= atoms
    valid_lane = (lane - jnp.where(upper, atoms, 0)) < jnp.where(upper, counts_ref[1], counts_ref[0])
    valid_row = valid_lane.astype(F32)

    place = 2.0 * jnp.concatenate(
        [jnp.concatenate([pos_ref[axis], pos_ref[3 + axis]], axis=-1) for axis in range(3)], axis=0
    )

    def packet_for(ox, oz):
        listed = [
            jnp.where(
                upper,
                mask_ref[1, direction(ox, -oy, oz)].astype(F32),
                mask_ref[0, direction(ox, -oy, oz)].astype(F32),
            )
            for oy in (-1, 0, 1)
        ]
        at = lax.rem(lane, atoms)
        row = jnp.where(at == 0, listed[0], jnp.where(at == 1, listed[1], listed[2]))
        return jnp.concatenate([place, row], axis=0)

    packet_in[0] = packet_for(0, 0)
    for slot, (column, level) in SLOTS.items():
        packet_out[slot] = packet_for(off_x[column], off_z[level])

    def held_at(kind, slot):
        return (packet_in, source, grads)[kind].at[slot]

    def remote(src, dst, send, recv, to):
        return pltpu.make_async_remote_copy(
            src_ref=src,
            dst_ref=dst,
            send_sem=send,
            recv_sem=recv,
            device_id=to,
            device_id_type=MESH,
        )

    def lands(kind, slot):
        if kind == 0:
            return slot - 1
        return 8 + (0, 1, 2, 3, 4, 5, 5, 6)[slot - 1]

    def landing(kind, slot):
        level = SLOTS[slot][1]
        if level == LEVEL:
            return recv_sem.at[lands(kind, slot)]
        column = SLOTS[slot][0]
        return recv_sem.at[jnp.where(into_z[level] == 3, lands(kind, 3 + column), lands(kind, 6 + column))]

    def spread(kind, slots):
        for slot in slots:
            column, level = SLOTS[slot]
            src = packet_out.at[slot] if kind == 0 else held_at(kind, 0)
            there = slot_there(slot)
            remote(src, held_at(kind, there), send_sem, landing(kind, slot), device(slot)).start()

    def arrived(kind, low, high):
        held = (packet_in, source, grads)[kind].at[low:high]
        remote(held, held, send_sem, recv_sem.at[lands(kind, low)], device(1)).wait_recv()

    def sent(kind, count):
        some = (packet_in, source, grads)[kind].at[0:count]
        remote(some, some, send_sem, recv_sem.at[0], device(1)).wait_send()

    def build(slot):
        column, level = SLOTS[slot] if slot else (SAME, LEVEL)
        ox, oz = off_x[column], off_z[level]
        packet = packet_in[slot]
        other_x = packet[0:1] + 2.0 * (ox if column == SAME else ox.astype(F32))
        other_y = packet[1:2]
        other_z = packet[2:3] + 2.0 * (oz if level == LEVEL else oz.astype(F32))
        theirs = [
            jnp.where(upper, packet[3:4, atoms + at : atoms + at + 1], packet[3:4, at : at + 1]) for at in range(3)
        ]
        chunk = 32
        half = bases // 2

        def step(first, gate_low, gate_high, move):
            some = slice(first, first + chunk)
            dx = other_x - own_cols[0, some, :]
            dy = other_y - own_cols[1, some, :]
            dz = other_z - own_cols[2, some, :]
            gate = jnp.where(dy > 0.0, gate_low, gate_high)
            dy = jnp.abs(dy) - move
            near = jnp.minimum(dx * dx + dy * dy + dz * dz, 1.0)
            room = 1.0 - near
            envelope = room * room * gate
            if slot == 0:
                at_row = lax.broadcasted_iota(jnp.int32, (chunk, rows), 0) + first
                at_lane = lax.broadcasted_iota(jnp.int32, (chunk, rows), 1)
                envelope = jnp.where(at_row == at_lane, 0.0, envelope)
            rise = (4.0 * LOG2E * bases) * near - (4.0 * LOG2E * half)
            up, down = jnp.exp2(rise), jnp.exp2(-rise)
            high = envelope * jnp.exp2(rise * (0.5 - rise * (0.125 / LOG2E)))
            low = high * down
            for step_out in range(half):
                if step_out:
                    high, low = high * up, low * down
                for b, value in ((half + step_out, high), (half - 1 - step_out, low)):
                    tiles[slot * bases + b, some, :] = value.astype(BF16)

        for c in range(2):
            cross = upper if c == 0 else jnp.logical_not(upper)
            low, same, high = (
                theirs[1 + oy] * mask_ref[c, direction(ox, oy, oz)].astype(F32) for oy in (-1, 0, 1)
            )
            gate_low = jnp.where(cross, low, same)
            gate_high = jnp.where(cross, high, same)
            move = jnp.where(cross, 2.0, 0.0)
            for first in range(c * atoms, (c + 1) * atoms, chunk):
                yield functools.partial(step, first, gate_low, gate_high, move)

    def gathered(slots, total, building=()):
        steps = [step for slot in building for step in build(slot)]
        values = jnp.concatenate([source[slot] for slot in slots], axis=1)
        for piece in range(PIECES):
            some = range(piece * bases // PIECES, (piece + 1) * bases // PIECES)
            built = [jnp.concatenate([tiles[slot * bases + b] for slot in slots], axis=1) for b in some]
            sums = nt(values, jnp.concatenate(built, axis=0))
            for at, b in enumerate(some):
                term = sums[:, at * rows : (at + 1) * rows] * weights[b]
                total = term if total is None else total + term
            for step in steps[piece * len(steps) // PIECES : (piece + 1) * len(steps) // PIECES]:
                step()
        return total

    def owed(value, slots):
        for slot in slots:
            built = tiles[pl.ds(slot * bases, bases)]
            some = jnp.concatenate([built[b] for b in range(bases)], axis=1)
            sums = jnp.dot(value, some, preferred_element_type=F32)
            total = None
            for b in range(bases):
                term = sums[:, b * rows : (b + 1) * rows] * weights[b]
                total = term if total is None else total + term
            owes[slot] = total.astype(BF16)

    def build_all(slot):
        for step in build(slot):
            step()

    fetched_pair(3)
    projected = nt(proj_ref[...], feat_ref[...])
    source[0] = (projected * valid_row).astype(BF16)

    heard = jnp.where(first_z, jnp.where(odd_x, 3, 1), jnp.where(second_z, 11, 8))

    @pl.when(here_z > 1)
    def _():
        with jax.named_scope("barrier"):
            pl.semaphore_wait(barrier, heard)
        spread(0, (2, 1, 8, 6, 7))
        spread(1, (2, 1, 8, 6, 7))
        spread(0, (5, 3, 4))
        spread(1, (5, 3, 4))

    with jax.named_scope("own"):
        columns = jnp.concatenate([place, jnp.zeros((5, rows), F32)], axis=0).T
        for axis in range(3):
            own_cols[axis] = jnp.broadcast_to(columns[:, axis : axis + 1], (rows, rows))
        fetches[5].wait()
        radial = (radial_ref[...] * basis_scale(bases)).T
        for b in range(bases):
            weights[b] = jnp.broadcast_to(radial[:, b : b + 1], (radial.shape[0], rows))
        fetched_pair(5)
        build_all(0)
        grad_act = nt(outw_ref[...], cot_ref[...])

    with jax.named_scope("spread"):

        @pl.when(first_z)
        def _():
            with jax.named_scope("barrier"):
                pl.semaphore_wait(barrier, heard)
            remote(packet_out.at[3:6], relay, send_sem, relay_sem, device(6)).start()
            spread(1, (6,))
            spread(0, (6,))

            @pl.when(odd_x)
            def _():
                for slot in (2, 1):
                    pl.semaphore_signal(told_sem.at[0], inc=1, device_id=device(slot), device_id_type=MESH)

            @pl.when(jnp.logical_not(odd_x))
            def _():
                pl.semaphore_wait(told_sem.at[0], 2)

            spread(0, (2, 1))
            spread(1, (2, 1))
            with jax.named_scope("told"):
                pl.semaphore_wait(told_sem.at[1], 1)
            spread(0, (8, 7))
            spread(1, (8, 7))

        @pl.when(second_z)
        def _():
            with jax.named_scope("barrier"):
                pl.semaphore_wait(barrier, heard)
            pl.semaphore_signal(told_sem.at[1], inc=1, device_id=device(3), device_id_type=MESH)
            spread(0, (2, 1, 3, 5, 4))
            spread(1, (2, 3, 5, 4, 1))

            def pass_on(kind, sources):
                for column in (OUTER, SAME, INNER):
                    there = 3 + column
                    land = recv_sem.at[lands(kind, there)]
                    to = (at_x[column], size_z - 1)
                    remote(sources[column], held_at(kind, there), send_sem, land, to).start()

            with jax.named_scope("relay"):
                remote(relay, relay, send_sem, relay_sem, device(1)).wait_recv()
            pass_on(0, [relay.at[column] for column in range(3)])
            with jax.named_scope("relay1"):
                arrived(1, 3, 4)
            pass_on(1, [held_at(1, 3)] * 3)
            spread(0, (8, 6, 7))
            spread(1, (8, 6, 7))

    def take(kind, slot):
        if kind == 0:
            arrived(0, slot, slot + 1)
        elif kind == 1 and slot == 3:
            pl.when(jnp.logical_not(second_z))(lambda: arrived(1, 3, 4))
        elif slot == 8 or lands(kind, slot + 1) != lands(kind, slot):
            low = min(at for at in range(1, 9) if lands(kind, at) == lands(kind, slot))
            arrived(kind, low, slot + 1)

    message = None
    for at, (packets, features, group) in enumerate(STAGES):
        with jax.named_scope(f"p{at}"):
            for slot in packets:
                take(0, slot)
        with jax.named_scope(f"s{at}"):
            for slot in features:
                take(1, slot)
        with jax.named_scope("stage"):
            if group:
                message = gathered(group, message, packets)
            else:
                for slot in packets:
                    build_all(slot)

    message = message * valid_row
    gate = 0.5 + 0.5 * jnp.tanh(0.5 * message)
    grad_msg = grad_act * gate * (1.0 + message * (1.0 - gate)) * valid_row
    grad_msg = grad_msg.astype(BF16)
    for turn in range(3):
        level = jnp.where(first_z, (0, 2, 1)[turn], jnp.where(last_z, (1, 2, 0)[turn], (1, 0, 2)[turn]))
        to_z = jnp.where(level == SOONER, at_z[SOONER], jnp.where(level == LATER, at_z[LATER], here_z))
        there_z = jnp.where(level == SOONER, into_z[SOONER], jnp.where(level == LATER, into_z[LATER], 0))
        land = recv_sem.at[15 + there_z // 3]
        with jax.named_scope(f"owed{turn}"):
            for columns in ((OUTER,), (SAME, INNER)) if turn == 0 else ((OUTER, SAME, INNER),):
                owed(grad_msg, [3 * level + column for column in columns])
                for column in columns:

                    def send(column=column):
                        src, dst = owes.at[3 * level + column], grads.at[there_z + column]
                        remote(src, dst, send_sem, land, (at_x[column], to_z)).start()

                    if column == SAME:
                        pl.when(level != LEVEL)(send)
                    else:
                        send()

    activated = (message * gate).astype(BF16)
    both_ref[0] = (feat_ref[...].astype(F32) + tn(activated, outw_ref[...])).astype(BF16)

    total = owes[0].astype(F32)
    for low, high in ((1, 3), (3, 6), (6, 9)):
        with jax.named_scope(f"g{high - 1}"):
            held = grads.at[low:high]
            remote(held, held, send_sem, recv_sem.at[15 + low // 3], device(1)).wait_recv()
        for slot in range(low, high):
            total += grads[slot].astype(F32)
    grad_proj = (total * valid_row).astype(BF16)
    pulled = tn(grad_proj, proj_ref[...])
    both_ref[1] = (cot_ref[...].astype(F32) + pulled).astype(BF16)

    with jax.named_scope("sent"):
        sent(0, 8)
        sent(1, 5)
        sent(2, 8)

        @pl.when(jnp.logical_not(first_z))
        def _():
            sent(1, 3)

        @pl.when(second_z)
        def _():
            sent(0, 3)
            sent(1, 3)


def on_device(
    features, cotangent, positions, counts, neighbour_mask, proj_weight, out_weight, radial_weight
):
    shape = features.shape
    cells, atoms, channels = shape[1], shape[3], shape[4]
    bases, width = radial_weight.shape
    rows = cells * atoms
    assert shape[0] == 1 and shape[2] == 1 and cells == 2
    operands = (
        features.reshape(rows, channels),
        cotangent.reshape(rows, channels),
        positions.reshape(cells * 3, 1, atoms),
        counts.reshape(cells),
        neighbour_mask.reshape(cells, neighbour_mask.shape[-1]),
        proj_weight.T,
        out_weight,
        radial_weight,
    )
    held = [pltpu.SMEM if at in (3, 4) else pltpu.VMEM for at in range(len(operands))]
    both = pl.pallas_call(
        functools.partial(kernel, atoms, bases),
        out_shape=pltpu.VMEM((2, rows, channels), BF16),
        in_specs=[pl.BlockSpec(memory_space=pl.ANY)] * len(operands),
        out_specs=pl.BlockSpec(memory_space=pltpu.VMEM),
        scratch_shapes=[space(x.shape, x.dtype) for space, x in zip(held, operands)]
        + [
            pltpu.VMEM((9, 4, rows), F32),
            pltpu.VMEM((9, 4, rows), F32),
            pltpu.VMEM((3, 4, rows), F32),
            pltpu.VMEM((3, rows, rows), F32),
            pltpu.VMEM((9 * bases, rows, rows), BF16),
            pltpu.VMEM((bases, width, rows), F32),
            pltpu.VMEM((9, width, rows), BF16),
            pltpu.VMEM((9, width, rows), BF16),
            pltpu.VMEM((9, width, rows), BF16),
            pltpu.SemaphoreType.DMA((6,)),
            pltpu.SemaphoreType.DMA,
            pltpu.SemaphoreType.REGULAR((2,)),
            pltpu.SemaphoreType.DMA,
            pltpu.SemaphoreType.DMA((18,)),
        ],
        compiler_params=pltpu.CompilerParams(collective_id=0, has_side_effects=True),
    )(*operands)
    return both[0].reshape(shape), both[1].reshape(shape)


def solution(mesh):
    cell = P("xy", None, "gz", None, None)
    return jax.shard_map(
        on_device,
        mesh=mesh,
        in_specs=(cell, cell, cell, P("xy", None, "gz"), P("xy", None, "gz", None), P(), P(), P()),
        out_specs=(cell, cell),
        check_vma=False,
    )
```

```python
import functools

import jax
import jax.numpy as jnp
from jax import lax
from jax.experimental import pallas as pl
from jax.experimental.pallas import tpu as pltpu
from jax.sharding import PartitionSpec as P

MESH = pl.DeviceIdType.MESH
AXES = ("xy", "gz")
F32 = jnp.float32
BF16 = jnp.bfloat16
LOG2E = 1.4426950408889634
FALL = 2.718281828459045**-4
PIECES = 4

SAME, INNER, OUTER = 0, 1, 2
LEVEL, SOONER, LATER = 0, 1, 2
SLOTS = {1: (INNER, LEVEL), 2: (OUTER, LEVEL)}
SLOTS.update({3 + at: (at, SOONER) for at in (SAME, INNER, OUTER)})
SLOTS.update({6 + at: (at, LATER) for at in (SAME, INNER, OUTER)})
STAGES = (
    ((1,), (), ()),
    ((2,), (1,), (0, 1)),
    ((6, 7), (2,), (2,)),
    ((8,), (), ()),
    ((3,), (6, 7), (6, 7)),
    ((), (3, 8), (3, 8)),
    ((4,), (), ()),
    ((5,), (), ()),
    ((), (4, 5), (4, 5)),
)


def nt(a, b):
    return lax.dot_general(a, b, (((1,), (1,)), ((), ())), preferred_element_type=F32)


def tn(a, b):
    return lax.dot_general(a, b, (((0,), (0,)), ((), ())), preferred_element_type=F32)


def direction(ox, oy, oz):
    return (ox + 1) * 9 + (oy + 1) * 3 + oz + 1


def kernel(
    atoms,
    bases,
    feat_hbm,
    cot_hbm,
    pos_hbm,
    counts_hbm,
    mask_hbm,
    proj_hbm,
    outw_hbm,
    radial_hbm,
    both_ref,
    feat_ref,
    cot_ref,
    pos_ref,
    counts_ref,
    mask_ref,
    proj_ref,
    outw_ref,
    radial_ref,
    packet_out,
    packet_in,
    relay,
    own_cols,
    tiles,
    weights,
    source,
    grads,
    owes,
    local_sem,
    relay_sem,
    told_sem,
    send_sem,
    recv_sem,
):
    rows = feat_ref.shape[0]
    size_x, size_z = [lax.axis_size(axis) for axis in AXES]
    assert size_x % 2 == 0 and size_z >= 4
    here_x, here_z = [lax.axis_index(axis) for axis in AXES]
    first_z, second_z, last_z = here_z == 0, here_z == 1, here_z == size_z - 1

    odd_x = lax.rem(here_x, 2) == 1
    inward = jnp.where(odd_x, -1, 1)
    off_x = (0, inward, -inward)

    def sooner_of(z):
        return jnp.where(z == size_z - 1, 1, -1)

    off_z = (0, sooner_of(here_z), -sooner_of(here_z))
    at_x = [here_x] + [lax.rem(here_x + off + size_x, size_x) for off in off_x[1:]]
    at_z = [here_z] + [lax.rem(here_z + off + size_z, size_z) for off in off_z[1:]]

    into_z = [0] + [
        jnp.where(sooner_of(at_z[side]) == -off_z[side], 3, 6) for side in (SOONER, LATER)
    ]

    def slot_there(slot):
        column, level = SLOTS[slot]
        return slot if level == LEVEL else into_z[level] + column

    def device(slot):
        column, level = SLOTS[slot]
        return (at_x[column], at_z[level])

    barrier = pltpu.get_barrier_semaphore()

    def greet(column, z):
        pl.semaphore_signal(barrier, inc=1, device_id=(at_x[column], z), device_id_type=MESH)

    sooner_z = jnp.where(last_z, 1, at_z[SOONER])

    @pl.when(jnp.logical_not(second_z))
    def _():
        greet(OUTER, sooner_z)
        greet(INNER, sooner_z)

    greet(SAME, sooner_z)
    for column in (OUTER, SAME, INNER):
        greet(column, at_z[LATER])

    @pl.when(jnp.logical_not(jnp.logical_and(first_z, odd_x)))
    def _():
        greet(OUTER, here_z)
        greet(INNER, here_z)

    fetches = [
        pltpu.make_async_copy(far, near, local_sem.at[at])
        for at, far, near in (
            (0, mask_hbm, mask_ref),
            (1, counts_hbm, counts_ref),
            (2, pos_hbm, pos_ref),
            (3, proj_hbm, proj_ref),
            (3, feat_hbm, feat_ref),
            (4, radial_hbm, radial_ref),
            (5, outw_hbm, outw_ref),
            (5, cot_hbm, cot_ref),
        )
    ]
    for fetch in fetches:
        fetch.start()

    def fetched_pair(at):
        both = source.at[0 : 1 + rows // proj_ref.shape[0]]
        pltpu.make_async_copy(both, both, local_sem.at[at]).wait()

    with jax.named_scope("fetch"):
        for fetch in fetches[:3]:
            fetch.wait()

    lane = lax.broadcasted_iota(jnp.int32, (1, rows), 1)
    upper = lane >= atoms
    valid_lane = (lane - jnp.where(upper, atoms, 0)) < jnp.where(upper, counts_ref[1], counts_ref[0])
    valid_row = valid_lane.astype(F32)

    place = 2.0 * jnp.concatenate(
        [jnp.concatenate([pos_ref[axis], pos_ref[3 + axis]], axis=-1) for axis in range(3)], axis=0
    )

    def packet_for(ox, oz):
        listed = [
            jnp.where(
                upper,
                mask_ref[1, direction(ox, -oy, oz)].astype(F32),
                mask_ref[0, direction(ox, -oy, oz)].astype(F32),
            )
            for oy in (-1, 0, 1)
        ]
        at = lax.rem(lane, atoms)
        row = jnp.where(at == 0, listed[0], jnp.where(at == 1, listed[1], listed[2]))
        return jnp.concatenate([place, row], axis=0)

    packet_in[0] = packet_for(0, 0)
    for slot, (column, level) in SLOTS.items():
        packet_out[slot] = packet_for(off_x[column], off_z[level])

    def held_at(kind, slot):
        return (packet_in, source, grads)[kind].at[slot]

    def remote(src, dst, send, recv, to):
        return pltpu.make_async_remote_copy(
            src_ref=src,
            dst_ref=dst,
            send_sem=send,
            recv_sem=recv,
            device_id=to,
            device_id_type=MESH,
        )

    def lands(kind, slot):
        if kind == 0:
            return (0, 1, 2, 3, 4, 5, 5, 6)[slot - 1]
        return 7 + (0, 1, 2, 3, 3, 4, 4, 5)[slot - 1]

    def landing(kind, slot):
        level = SLOTS[slot][1]
        if level == LEVEL:
            return recv_sem.at[lands(kind, slot)]
        column = SLOTS[slot][0]
        return recv_sem.at[jnp.where(into_z[level] == 3, lands(kind, 3 + column), lands(kind, 6 + column))]

    def spread(kind, slots):
        for slot in slots:
            column, level = SLOTS[slot]
            src = packet_out.at[slot] if kind == 0 else held_at(kind, 0)
            there = slot_there(slot)
            remote(src, held_at(kind, there), send_sem, landing(kind, slot), device(slot)).start()

    def arrived(kind, low, high):
        held = (packet_in, source, grads)[kind].at[low:high]
        remote(held, held, send_sem, recv_sem.at[lands(kind, low)], device(1)).wait_recv()

    def sent(kind, count):
        some = (packet_in, source, grads)[kind].at[0:count]
        remote(some, some, send_sem, recv_sem.at[0], device(1)).wait_send()

    def build(slot):
        column, level = SLOTS[slot] if slot else (SAME, LEVEL)
        ox, oz = off_x[column], off_z[level]
        packet = packet_in[slot]
        other_x = packet[0:1] + 2.0 * (ox if column == SAME else ox.astype(F32))
        other_y = packet[1:2]
        other_z = packet[2:3] + 2.0 * (oz if level == LEVEL else oz.astype(F32))
        theirs = [
            jnp.where(upper, packet[3:4, atoms + at : atoms + at + 1], packet[3:4, at : at + 1]) for at in range(3)
        ]
        chunk = 32
        half = bases // 2

        def step(first, gate_low, gate_high, move):
            some = slice(first, first + chunk)
            dx = other_x - own_cols[0, some, :]
            dy = other_y - own_cols[1, some, :]
            dz = other_z - own_cols[2, some, :]
            gate = jnp.where(dy > 0.0, gate_low, gate_high)
            dy = jnp.abs(dy) - move
            near = jnp.minimum(dx * dx + dy * dy + dz * dz, 1.0)
            room = 1.0 - near
            envelope = room * room * gate
            if slot == 0:
                at_row = lax.broadcasted_iota(jnp.int32, (chunk, rows), 0) + first
                at_lane = lax.broadcasted_iota(jnp.int32, (chunk, rows), 1)
                envelope = jnp.where(at_row == at_lane, 0.0, envelope)
            rise = (4.0 * LOG2E * bases) * near - (4.0 * LOG2E * half)
            up, down = jnp.exp2(rise), jnp.exp2(-rise)
            high = envelope * jnp.exp2(rise * (0.5 - rise * (0.125 / LOG2E)) - 0.5 * LOG2E)
            low = high * down
            for step_out in range(half):
                if step_out:
                    up, down = up * FALL, down * FALL
                    high, low = high * up, low * down
                for b, value in ((half + step_out, high), (half - 1 - step_out, low)):
                    tiles[slot * bases + b, some, :] = value.astype(BF16)

        for c in range(2):
            cross = upper if c == 0 else jnp.logical_not(upper)
            low, same, high = (
                theirs[1 + oy] * mask_ref[c, direction(ox, oy, oz)].astype(F32) for oy in (-1, 0, 1)
            )
            gate_low = jnp.where(cross, low, same)
            gate_high = jnp.where(cross, high, same)
            move = jnp.where(cross, 2.0, 0.0)
            for first in range(c * atoms, (c + 1) * atoms, chunk):
                yield functools.partial(step, first, gate_low, gate_high, move)

    def gathered(slots, total, building=()):
        steps = [step for slot in building for step in build(slot)]
        values = jnp.concatenate([source[slot] for slot in slots], axis=1)
        for piece in range(PIECES):
            some = range(piece * bases // PIECES, (piece + 1) * bases // PIECES)
            built = [jnp.concatenate([tiles[slot * bases + b] for slot in slots], axis=1) for b in some]
            sums = nt(values, jnp.concatenate(built, axis=0))
            for at, b in enumerate(some):
                term = sums[:, at * rows : (at + 1) * rows] * weights[b]
                total = term if total is None else total + term
            for step in steps[piece * len(steps) // PIECES : (piece + 1) * len(steps) // PIECES]:
                step()
        return total

    def owed(value, slots):
        for slot in slots:
            built = tiles[pl.ds(slot * bases, bases)]
            some = jnp.concatenate([built[b] for b in range(bases)], axis=1)
            sums = jnp.dot(value, some, preferred_element_type=F32)
            total = None
            for b in range(bases):
                term = sums[:, b * rows : (b + 1) * rows] * weights[b]
                total = term if total is None else total + term
            owes[slot] = total.astype(BF16)

    def build_all(slot):
        for step in build(slot):
            step()

    fetched_pair(3)
    projected = nt(proj_ref[...], feat_ref[...])
    source[0] = (projected * valid_row).astype(BF16)

    heard = jnp.where(first_z, jnp.where(odd_x, 3, 1), jnp.where(second_z, 11, 8))

    @pl.when(here_z > 1)
    def _():
        with jax.named_scope("barrier"):
            pl.semaphore_wait(barrier, heard)
        spread(0, (2, 1, 8, 6, 7))
        spread(1, (2, 1, 8, 6, 7))
        spread(0, (5, 3, 4))
        spread(1, (5, 3, 4))

    with jax.named_scope("own"):
        columns = jnp.concatenate([place, jnp.zeros((5, rows), F32)], axis=0).T
        for axis in range(3):
            own_cols[axis] = jnp.broadcast_to(columns[:, axis : axis + 1], (rows, rows))
        fetches[5].wait()
        radial = radial_ref[...].T
        for b in range(bases):
            weights[b] = jnp.broadcast_to(radial[:, b : b + 1], (radial.shape[0], rows))
        fetched_pair(5)
        build_all(0)
        grad_act = nt(outw_ref[...], cot_ref[...])

    with jax.named_scope("spread"):

        @pl.when(first_z)
        def _():
            with jax.named_scope("barrier"):
                pl.semaphore_wait(barrier, heard)
            remote(packet_out.at[3:6], relay, send_sem, relay_sem, device(6)).start()
            spread(1, (6,))
            spread(0, (6,))

            @pl.when(odd_x)
            def _():
                for slot in (2, 1):
                    pl.semaphore_signal(told_sem.at[0], inc=1, device_id=device(slot), device_id_type=MESH)

            @pl.when(jnp.logical_not(odd_x))
            def _():
                pl.semaphore_wait(told_sem.at[0], 2)

            spread(0, (2, 1))
            spread(1, (2, 1))
            with jax.named_scope("told"):
                pl.semaphore_wait(told_sem.at[1], 1)
            spread(0, (8, 7))
            spread(1, (8, 7))

        @pl.when(second_z)
        def _():
            with jax.named_scope("barrier"):
                pl.semaphore_wait(barrier, heard)
            pl.semaphore_signal(told_sem.at[1], inc=1, device_id=device(3), device_id_type=MESH)
            spread(0, (2, 1, 3, 5, 4))

            def pass_on(kind, sources):
                for column in (OUTER, SAME, INNER):
                    there = 3 + column
                    land = recv_sem.at[lands(kind, there)]
                    to = (at_x[column], size_z - 1)
                    remote(sources[column], held_at(kind, there), send_sem, land, to).start()

            with jax.named_scope("relay"):
                remote(relay, relay, send_sem, relay_sem, device(1)).wait_recv()
            pass_on(0, [relay.at[column] for column in range(3)])
            with jax.named_scope("relay1"):
                arrived(1, 3, 4)
            pass_on(1, [held_at(1, 3)] * 3)
            spread(1, (2, 3, 5, 4, 1))
            spread(0, (8, 6, 7))
            spread(1, (8, 6, 7))

    def take(kind, slot):
        if kind == 1 and slot == 3:
            pl.when(jnp.logical_not(second_z))(lambda: arrived(1, 3, 4))
        elif slot == 8 or lands(kind, slot + 1) != lands(kind, slot):
            low = min(at for at in range(1, 9) if lands(kind, at) == lands(kind, slot))
            arrived(kind, low, slot + 1)

    message = None
    for at, (packets, features, group) in enumerate(STAGES):
        with jax.named_scope(f"p{at}"):
            for slot in packets:
                take(0, slot)
        with jax.named_scope(f"s{at}"):
            for slot in features:
                take(1, slot)
        with jax.named_scope("stage"):
            if group:
                message = gathered(group, message, packets)
            else:
                for slot in packets:
                    build_all(slot)

    message = message * valid_row
    gate = 0.5 + 0.5 * jnp.tanh(0.5 * message)
    grad_msg = grad_act * gate * (1.0 + message * (1.0 - gate)) * valid_row
    grad_msg = grad_msg.astype(BF16)
    for turn in range(3):
        level = jnp.where(last_z, (1, 2, 0)[turn], jnp.where(second_z, (1, 0, 2)[turn], (0, 2, 1)[turn]))
        to_z = jnp.where(level == SOONER, at_z[SOONER], jnp.where(level == LATER, at_z[LATER], here_z))
        there_z = jnp.where(level == SOONER, into_z[SOONER], jnp.where(level == LATER, into_z[LATER], 0))
        land = recv_sem.at[13 + there_z // 3]
        with jax.named_scope(f"owed{turn}"):
            for columns in ((OUTER,), (SAME, INNER)) if turn == 0 else ((OUTER, SAME, INNER),):
                owed(grad_msg, [3 * level + column for column in columns])
                for column in columns:

                    def send(column=column):
                        src, dst = owes.at[3 * level + column], grads.at[there_z + column]
                        remote(src, dst, send_sem, land, (at_x[column], to_z)).start()

                    if column == SAME:
                        pl.when(level != LEVEL)(send)
                    else:
                        send()

    activated = (message * gate).astype(BF16)
    both_ref[0] = (feat_ref[...].astype(F32) + tn(activated, outw_ref[...])).astype(BF16)

    total = owes[0].astype(F32)
    for low, high in ((1, 3), (3, 6), (6, 9)):
        with jax.named_scope(f"g{high - 1}"):
            held = grads.at[low:high]
            remote(held, held, send_sem, recv_sem.at[13 + low // 3], device(1)).wait_recv()
        for slot in range(low, high):
            total += grads[slot].astype(F32)
    grad_proj = (total * valid_row).astype(BF16)
    pulled = tn(grad_proj, proj_ref[...])
    both_ref[1] = (cot_ref[...].astype(F32) + pulled).astype(BF16)

    with jax.named_scope("sent"):
        sent(0, 8)
        sent(1, 5)
        sent(2, 8)

        @pl.when(jnp.logical_not(first_z))
        def _():
            sent(1, 3)

        @pl.when(second_z)
        def _():
            sent(0, 3)
            sent(1, 3)


def on_device(
    features, cotangent, positions, counts, neighbour_mask, proj_weight, out_weight, radial_weight
):
    shape = features.shape
    cells, atoms, channels = shape[1], shape[3], shape[4]
    bases, width = radial_weight.shape
    rows = cells * atoms
    assert shape[0] == 1 and shape[2] == 1 and cells == 2
    operands = (
        features.reshape(rows, channels),
        cotangent.reshape(rows, channels),
        positions.reshape(cells * 3, 1, atoms),
        counts.reshape(cells),
        neighbour_mask.reshape(cells, neighbour_mask.shape[-1]),
        proj_weight.T,
        out_weight,
        radial_weight,
    )
    held = [pltpu.SMEM if at in (3, 4) else pltpu.VMEM for at in range(len(operands))]
    both = pl.pallas_call(
        functools.partial(kernel, atoms, bases),
        out_shape=pltpu.VMEM((2, rows, channels), BF16),
        in_specs=[pl.BlockSpec(memory_space=pl.ANY)] * len(operands),
        out_specs=pl.BlockSpec(memory_space=pltpu.VMEM),
        scratch_shapes=[space(x.shape, x.dtype) for space, x in zip(held, operands)]
        + [
            pltpu.VMEM((9, 4, rows), F32),
            pltpu.VMEM((9, 4, rows), F32),
            pltpu.VMEM((3, 4, rows), F32),
            pltpu.VMEM((3, rows, rows), F32),
            pltpu.VMEM((9 * bases, rows, rows), BF16),
            pltpu.VMEM((bases, width, rows), F32),
            pltpu.VMEM((9, width, rows), BF16),
            pltpu.VMEM((9, width, rows), BF16),
            pltpu.VMEM((9, width, rows), BF16),
            pltpu.SemaphoreType.DMA((6,)),
            pltpu.SemaphoreType.DMA,
            pltpu.SemaphoreType.REGULAR((2,)),
            pltpu.SemaphoreType.DMA,
            pltpu.SemaphoreType.DMA((16,)),
        ],
        compiler_params=pltpu.CompilerParams(collective_id=0, has_side_effects=True),
    )(*operands)
    return both[0].reshape(shape), both[1].reshape(shape)


def solution(mesh):
    cell = P("xy", None, "gz", None, None)
    return jax.shard_map(
        on_device,
        mesh=mesh,
        in_specs=(cell, cell, cell, P("xy", None, "gz"), P("xy", None, "gz", None), P(), P(), P()),
        out_specs=(cell, cell),
        check_vma=False,
    )
```

```python
import functools

import jax
import jax.numpy as jnp
from jax import lax
from jax.experimental import pallas as pl
from jax.experimental.pallas import tpu as pltpu
from jax.sharding import PartitionSpec as P

MESH = pl.DeviceIdType.MESH
AXES = ("xy", "gz")
F32 = jnp.float32
BF16 = jnp.bfloat16
LOG2E = 1.4426950408889634
FALL = 2.718281828459045**-4
PIECES = 4

SAME, INNER, OUTER = 0, 1, 2
LEVEL, SOONER, LATER = 0, 1, 2
SLOTS = {1: (INNER, LEVEL), 2: (OUTER, LEVEL)}
SLOTS.update({3 + at: (at, SOONER) for at in (SAME, INNER, OUTER)})
SLOTS.update({6 + at: (at, LATER) for at in (SAME, INNER, OUTER)})
STAGES = (
    ((1,), (), ()),
    ((2,), (1,), (0, 1)),
    ((6, 7), (2,), (2,)),
    ((8,), (), ()),
    ((3,), (6, 7), (6, 7)),
    ((), (3, 8), (3, 8)),
    ((4,), (), ()),
    ((5,), (), ()),
    ((), (4, 5), (4, 5)),
)


def nt(a, b):
    return lax.dot_general(a, b, (((1,), (1,)), ((), ())), preferred_element_type=F32)


def tn(a, b):
    return lax.dot_general(a, b, (((0,), (0,)), ((), ())), preferred_element_type=F32)


def direction(ox, oy, oz):
    return (ox + 1) * 9 + (oy + 1) * 3 + oz + 1


def kernel(
    atoms,
    bases,
    feat_hbm,
    cot_hbm,
    pos_hbm,
    counts_hbm,
    mask_hbm,
    proj_hbm,
    outw_hbm,
    radial_hbm,
    both_ref,
    feat_ref,
    cot_ref,
    pos_ref,
    counts_ref,
    mask_ref,
    proj_ref,
    outw_ref,
    radial_ref,
    packet_out,
    packet_in,
    relay,
    own_cols,
    tiles,
    weights,
    source,
    grads,
    owes,
    local_sem,
    relay_sem,
    told_sem,
    send_sem,
    recv_sem,
):
    rows = feat_ref.shape[0]
    size_x, size_z = [lax.axis_size(axis) for axis in AXES]
    assert size_x % 2 == 0 and size_z >= 4
    here_x, here_z = [lax.axis_index(axis) for axis in AXES]
    first_z, second_z, last_z = here_z == 0, here_z == 1, here_z == size_z - 1

    odd_x = lax.rem(here_x, 2) == 1
    inward = jnp.where(odd_x, -1, 1)
    off_x = (0, inward, -inward)

    def sooner_of(z):
        return jnp.where(z == size_z - 1, 1, -1)

    off_z = (0, sooner_of(here_z), -sooner_of(here_z))
    at_x = [here_x] + [lax.rem(here_x + off + size_x, size_x) for off in off_x[1:]]
    at_z = [here_z] + [lax.rem(here_z + off + size_z, size_z) for off in off_z[1:]]

    into_z = [0] + [
        jnp.where(sooner_of(at_z[side]) == -off_z[side], 3, 6) for side in (SOONER, LATER)
    ]

    def slot_there(slot):
        column, level = SLOTS[slot]
        return slot if level == LEVEL else into_z[level] + column

    def device(slot):
        column, level = SLOTS[slot]
        return (at_x[column], at_z[level])

    barrier = pltpu.get_barrier_semaphore()

    def greet(column, z):
        pl.semaphore_signal(barrier, inc=1, device_id=(at_x[column], z), device_id_type=MESH)

    sooner_z = jnp.where(last_z, 1, at_z[SOONER])

    @pl.when(jnp.logical_not(second_z))
    def _():
        greet(OUTER, sooner_z)
        greet(INNER, sooner_z)

    greet(SAME, sooner_z)
    for column in (OUTER, SAME, INNER):
        greet(column, at_z[LATER])

    @pl.when(jnp.logical_not(jnp.logical_and(first_z, odd_x)))
    def _():
        greet(OUTER, here_z)
        greet(INNER, here_z)

    fetches = [
        pltpu.make_async_copy(far, near, local_sem.at[at])
        for at, far, near in (
            (0, mask_hbm, mask_ref),
            (1, counts_hbm, counts_ref),
            (2, pos_hbm, pos_ref),
            (3, proj_hbm, proj_ref),
            (3, feat_hbm, feat_ref),
            (4, radial_hbm, radial_ref),
            (5, outw_hbm, outw_ref),
            (5, cot_hbm, cot_ref),
        )
    ]
    for fetch in fetches:
        fetch.start()

    def fetched_pair(at):
        both = source.at[0 : 1 + rows // proj_ref.shape[0]]
        pltpu.make_async_copy(both, both, local_sem.at[at]).wait()

    with jax.named_scope("fetch"):
        for fetch in fetches[:3]:
            fetch.wait()

    lane = lax.broadcasted_iota(jnp.int32, (1, rows), 1)
    upper = lane >= atoms
    valid_lane = (lane - jnp.where(upper, atoms, 0)) < jnp.where(upper, counts_ref[1], counts_ref[0])
    valid_row = valid_lane.astype(F32)

    place = 2.0 * jnp.concatenate(
        [jnp.concatenate([pos_ref[axis], pos_ref[3 + axis]], axis=-1) for axis in range(3)], axis=0
    )

    def packet_for(ox, oz):
        listed = [
            jnp.where(
                upper,
                mask_ref[1, direction(ox, -oy, oz)].astype(F32),
                mask_ref[0, direction(ox, -oy, oz)].astype(F32),
            )
            for oy in (-1, 0, 1)
        ]
        at = lax.rem(lane, atoms)
        row = jnp.where(at == 0, listed[0], jnp.where(at == 1, listed[1], listed[2]))
        return jnp.concatenate([place, row], axis=0)

    packet_in[0] = packet_for(0, 0)
    for slot, (column, level) in SLOTS.items():
        packet_out[slot] = packet_for(off_x[column], off_z[level])

    def held_at(kind, slot):
        return (packet_in, source, grads)[kind].at[slot]

    def remote(src, dst, send, recv, to):
        return pltpu.make_async_remote_copy(
            src_ref=src,
            dst_ref=dst,
            send_sem=send,
            recv_sem=recv,
            device_id=to,
            device_id_type=MESH,
        )

    def lands(kind, slot):
        if kind == 0:
            return (0, 1, 2, 3, 4, 5, 5, 6)[slot - 1]
        return 7 + (0, 1, 2, 3, 3, 4, 4, 5)[slot - 1]

    def landing(kind, slot):
        level = SLOTS[slot][1]
        if level == LEVEL:
            return recv_sem.at[lands(kind, slot)]
        column = SLOTS[slot][0]
        return recv_sem.at[jnp.where(into_z[level] == 3, lands(kind, 3 + column), lands(kind, 6 + column))]

    def spread(kind, slots):
        for slot in slots:
            column, level = SLOTS[slot]
            src = packet_out.at[slot] if kind == 0 else held_at(kind, 0)
            there = slot_there(slot)
            remote(src, held_at(kind, there), send_sem, landing(kind, slot), device(slot)).start()

    def arrived(kind, low, high):
        held = (packet_in, source, grads)[kind].at[low:high]
        remote(held, held, send_sem, recv_sem.at[lands(kind, low)], device(1)).wait_recv()

    def sent(kind, count):
        some = (packet_in, source, grads)[kind].at[0:count]
        remote(some, some, send_sem, recv_sem.at[0], device(1)).wait_send()

    def build(slot):
        column, level = SLOTS[slot] if slot else (SAME, LEVEL)
        ox, oz = off_x[column], off_z[level]
        packet = packet_in[slot]
        other_x = packet[0:1] + 2.0 * (ox if column == SAME else ox.astype(F32))
        other_y = packet[1:2]
        other_z = packet[2:3] + 2.0 * (oz if level == LEVEL else oz.astype(F32))
        theirs = [
            jnp.where(upper, packet[3:4, atoms + at : atoms + at + 1], packet[3:4, at : at + 1]) for at in range(3)
        ]
        chunk = 16
        half = bases // 2

        def step(first, gate_low, gate_high, move):
            some = slice(first, first + chunk)
            dx = other_x - own_cols[0, some, :]
            dy = other_y - own_cols[1, some, :]
            dz = other_z - own_cols[2, some, :]
            gate = jnp.where(dy > 0.0, gate_low, gate_high)
            dy = jnp.abs(dy) - move
            near = jnp.minimum(dx * dx + dy * dy + dz * dz, 1.0)
            room = 1.0 - near
            envelope = room * room * gate
            if slot == 0:
                at_row = lax.broadcasted_iota(jnp.int32, (chunk, rows), 0) + first
                at_lane = lax.broadcasted_iota(jnp.int32, (chunk, rows), 1)
                envelope = jnp.where(at_row == at_lane, 0.0, envelope)
            rise = (4.0 * LOG2E * bases) * near - (4.0 * LOG2E * half)
            up, down = jnp.exp2(rise), jnp.exp2(-rise)
            high = envelope * jnp.exp2(rise * (0.5 - rise * (0.125 / LOG2E)) - 0.5 * LOG2E)
            low = high * down
            for step_out in range(half):
                if step_out:
                    up, down = up * FALL, down * FALL
                    high, low = high * up, low * down
                for b, value in ((half + step_out, high), (half - 1 - step_out, low)):
                    tiles[slot * bases + b, some, :] = value.astype(BF16)

        for c in range(2):
            cross = upper if c == 0 else jnp.logical_not(upper)
            low, same, high = (
                theirs[1 + oy] * mask_ref[c, direction(ox, oy, oz)].astype(F32) for oy in (-1, 0, 1)
            )
            gate_low = jnp.where(cross, low, same)
            gate_high = jnp.where(cross, high, same)
            move = jnp.where(cross, 2.0, 0.0)
            for first in range(c * atoms, (c + 1) * atoms, chunk):
                yield functools.partial(step, first, gate_low, gate_high, move)

    def gathered(slots, total, building=()):
        steps = [step for slot in building for step in build(slot)]
        values = jnp.concatenate([source[slot] for slot in slots], axis=1)
        for piece in range(PIECES):
            some = range(piece * bases // PIECES, (piece + 1) * bases // PIECES)
            built = [jnp.concatenate([tiles[slot * bases + b] for slot in slots], axis=1) for b in some]
            sums = nt(values, jnp.concatenate(built, axis=0))
            for at, b in enumerate(some):
                term = sums[:, at * rows : (at + 1) * rows] * weights[b]
                total = term if total is None else total + term
            for step in steps[piece * len(steps) // PIECES : (piece + 1) * len(steps) // PIECES]:
                step()
        return total

    def owed(value, slots):
        for slot in slots:
            built = tiles[pl.ds(slot * bases, bases)]
            some = jnp.concatenate([built[b] for b in range(bases)], axis=1)
            sums = jnp.dot(value, some, preferred_element_type=F32)
            total = None
            for b in range(bases):
                term = sums[:, b * rows : (b + 1) * rows] * weights[b]
                total = term if total is None else total + term
            owes[slot] = total.astype(BF16)

    def build_all(slot):
        for step in build(slot):
            step()

    fetched_pair(3)
    projected = nt(proj_ref[...], feat_ref[...])
    source[0] = (projected * valid_row).astype(BF16)

    heard = jnp.where(first_z, jnp.where(odd_x, 3, 1), jnp.where(second_z, 11, 8))

    @pl.when(here_z > 1)
    def _():
        with jax.named_scope("barrier"):
            pl.semaphore_wait(barrier, heard)
        spread(0, (2, 1, 8, 6, 7))
        spread(1, (2, 1, 8, 6, 7))
        spread(0, (5, 3, 4))
        spread(1, (5, 3, 4))

    with jax.named_scope("own"):
        columns = jnp.concatenate([place, jnp.zeros((5, rows), F32)], axis=0).T
        for axis in range(3):
            own_cols[axis] = jnp.broadcast_to(columns[:, axis : axis + 1], (rows, rows))
        fetches[5].wait()
        radial = radial_ref[...].T
        for b in range(bases):
            weights[b] = jnp.broadcast_to(radial[:, b : b + 1], (radial.shape[0], rows))
        fetched_pair(5)
        build_all(0)
        grad_act = nt(outw_ref[...], cot_ref[...])

    with jax.named_scope("spread"):

        @pl.when(first_z)
        def _():
            with jax.named_scope("barrier"):
                pl.semaphore_wait(barrier, heard)
            remote(packet_out.at[3:6], relay, send_sem, relay_sem, device(6)).start()
            spread(1, (6,))
            spread(0, (6,))

            @pl.when(odd_x)
            def _():
                for slot in (2, 1):
                    pl.semaphore_signal(told_sem.at[0], inc=1, device_id=device(slot), device_id_type=MESH)

            @pl.when(jnp.logical_not(odd_x))
            def _():
                pl.semaphore_wait(told_sem.at[0], 2)

            spread(0, (2, 1))
            spread(1, (2, 1))
            with jax.named_scope("told"):
                pl.semaphore_wait(told_sem.at[1], 1)
            spread(0, (8, 7))
            spread(1, (8, 7))

        @pl.when(second_z)
        def _():
            with jax.named_scope("barrier"):
                pl.semaphore_wait(barrier, heard)
            pl.semaphore_signal(told_sem.at[1], inc=1, device_id=device(3), device_id_type=MESH)
            spread(0, (2, 1, 3, 5, 4))

            def pass_on(kind, sources):
                for column in (OUTER, SAME, INNER):
                    there = 3 + column
                    land = recv_sem.at[lands(kind, there)]
                    to = (at_x[column], size_z - 1)
                    remote(sources[column], held_at(kind, there), send_sem, land, to).start()

            with jax.named_scope("relay"):
                remote(relay, relay, send_sem, relay_sem, device(1)).wait_recv()
            pass_on(0, [relay.at[column] for column in range(3)])
            with jax.named_scope("relay1"):
                arrived(1, 3, 4)
            pass_on(1, [held_at(1, 3)] * 3)
            spread(1, (2, 3, 5, 4, 1))
            spread(0, (8, 6, 7))
            spread(1, (8, 6, 7))

    def take(kind, slot):
        if kind == 1 and slot == 3:
            pl.when(jnp.logical_not(second_z))(lambda: arrived(1, 3, 4))
        elif slot == 8 or lands(kind, slot + 1) != lands(kind, slot):
            low = min(at for at in range(1, 9) if lands(kind, at) == lands(kind, slot))
            arrived(kind, low, slot + 1)

    message = None
    for at, (packets, features, group) in enumerate(STAGES):
        with jax.named_scope(f"p{at}"):
            for slot in packets:
                take(0, slot)
        with jax.named_scope(f"s{at}"):
            for slot in features:
                take(1, slot)
        with jax.named_scope("stage"):
            if group:
                message = gathered(group, message, packets)
            else:
                for slot in packets:
                    build_all(slot)

    message = message * valid_row
    gate = 0.5 + 0.5 * jnp.tanh(0.5 * message)
    grad_msg = grad_act * gate * (1.0 + message * (1.0 - gate)) * valid_row
    grad_msg = grad_msg.astype(BF16)
    for turn in range(3):
        level = jnp.where(last_z, (1, 0, 2)[turn], jnp.where(second_z, (1, 0, 2)[turn], (0, 2, 1)[turn]))
        to_z = jnp.where(level == SOONER, at_z[SOONER], jnp.where(level == LATER, at_z[LATER], here_z))
        there_z = jnp.where(level == SOONER, into_z[SOONER], jnp.where(level == LATER, into_z[LATER], 0))
        land = recv_sem.at[13 + there_z // 3]
        with jax.named_scope(f"owed{turn}"):
            for columns in ((OUTER,), (SAME, INNER)) if turn == 0 else ((OUTER, SAME, INNER),):
                owed(grad_msg, [3 * level + column for column in columns])
                for column in columns:

                    def send(column=column):
                        src, dst = owes.at[3 * level + column], grads.at[there_z + column]
                        remote(src, dst, send_sem, land, (at_x[column], to_z)).start()

                    if column == SAME:
                        pl.when(level != LEVEL)(send)
                    else:
                        send()

    activated = (message * gate).astype(BF16)
    both_ref[0] = (feat_ref[...].astype(F32) + tn(activated, outw_ref[...])).astype(BF16)

    total = owes[0].astype(F32)
    for low, high in ((1, 3), (3, 6), (6, 9)):
        with jax.named_scope(f"g{high - 1}"):
            held = grads.at[low:high]
            remote(held, held, send_sem, recv_sem.at[13 + low // 3], device(1)).wait_recv()
        for slot in range(low, high):
            total += grads[slot].astype(F32)
    grad_proj = (total * valid_row).astype(BF16)
    pulled = tn(grad_proj, proj_ref[...])
    both_ref[1] = (cot_ref[...].astype(F32) + pulled).astype(BF16)

    with jax.named_scope("sent"):
        sent(0, 8)
        sent(1, 5)
        sent(2, 8)

        @pl.when(jnp.logical_not(first_z))
        def _():
            sent(1, 3)

        @pl.when(second_z)
        def _():
            sent(0, 3)
            sent(1, 3)


def on_device(
    features, cotangent, positions, counts, neighbour_mask, proj_weight, out_weight, radial_weight
):
    shape = features.shape
    cells, atoms, channels = shape[1], shape[3], shape[4]
    bases, width = radial_weight.shape
    rows = cells * atoms
    assert shape[0] == 1 and shape[2] == 1 and cells == 2
    operands = (
        features.reshape(rows, channels),
        cotangent.reshape(rows, channels),
        positions.reshape(cells * 3, 1, atoms),
        counts.reshape(cells),
        neighbour_mask.reshape(cells, neighbour_mask.shape[-1]),
        proj_weight.T,
        out_weight,
        radial_weight,
    )
    held = [pltpu.SMEM if at in (3, 4) else pltpu.VMEM for at in range(len(operands))]
    both = pl.pallas_call(
        functools.partial(kernel, atoms, bases),
        out_shape=pltpu.VMEM((2, rows, channels), BF16),
        in_specs=[pl.BlockSpec(memory_space=pl.ANY)] * len(operands),
        out_specs=pl.BlockSpec(memory_space=pltpu.VMEM),
        scratch_shapes=[space(x.shape, x.dtype) for space, x in zip(held, operands)]
        + [
            pltpu.VMEM((9, 4, rows), F32),
            pltpu.VMEM((9, 4, rows), F32),
            pltpu.VMEM((3, 4, rows), F32),
            pltpu.VMEM((3, rows, rows), F32),
            pltpu.VMEM((9 * bases, rows, rows), BF16),
            pltpu.VMEM((bases, width, rows), F32),
            pltpu.VMEM((9, width, rows), BF16),
            pltpu.VMEM((9, width, rows), BF16),
            pltpu.VMEM((9, width, rows), BF16),
            pltpu.SemaphoreType.DMA((6,)),
            pltpu.SemaphoreType.DMA,
            pltpu.SemaphoreType.REGULAR((2,)),
            pltpu.SemaphoreType.DMA,
            pltpu.SemaphoreType.DMA((16,)),
        ],
        compiler_params=pltpu.CompilerParams(collective_id=0, has_side_effects=True),
    )(*operands)
    return both[0].reshape(shape), both[1].reshape(shape)


def solution(mesh):
    cell = P("xy", None, "gz", None, None)
    return jax.shard_map(
        on_device,
        mesh=mesh,
        in_specs=(cell, cell, cell, P("xy", None, "gz"), P("xy", None, "gz", None), P(), P(), P()),
        out_specs=(cell, cell),
        check_vma=False,
    )
```
